512 devices in a mesh: dom: 64 (over z, x_lo, core), bin: 8 (over y, x_hi).
Axes of the slice: x: 4 (x_hi: 2, x_lo: 2; x = x_hi * 2 + x_lo), y: 4, z: 16, core: 2. Of those that a mesh axis runs over, the one named last changes fastest.
Arguments:
- dust_rho: float32 [128, 65536], P('bin', 'dom'), may hold values from 0.25 to 4
- dust_vel: float32 [2, 128, 65536], P(None, 'bin', 'dom'), may hold values from -4 to 4
- gas_rho: float32 [65536], P('dom'), may hold values from 50 to 500
- gas_vel: float32 [2, 65536], P(None, 'dom'), may hold values from -4 to 4
- normals: float32 [2, 8, 65536], P(None, None, 'dom'), may hold values from -0.24 to 0.24
- inv_volume: float32 [65536], P('dom'), may hold values from 0.75 to 3
- coag_rate: float32 [65536], P('dom'), may hold values from 0.03 to 0.3
- drag_coef: float32 [128], P('bin'), as said below
- neighbours: int32 [8, 65536], P(None, 'dom'), may hold values from -1 to 1535, as said below
- send_cells: int32 [64, 4, 128], P('dom'), may hold values from -1 to 1023, as said below
- kernel: bfloat16 [128, 128], replicated, may hold values from 0.001953125 to 0.0703125, as said below
- redistrib: bfloat16 [128, 128], replicated, may hold values from -0.5 to 0.5
Outputs:
- dust_rho_out: float32 [128, 65536], P('bin', 'dom')
- dust_vel_out: float32 [2, 128, 65536], P(None, 'bin', 'dom')
- gas_vel_out: float32 [2, 65536], P(None, 'dom')
The draws below stay inside these ranges and needn't reach their ends.
Inputs may be any that keep to these rules, and one draw needn't show every extreme that they name: Row send_cells[d, j] lists distinct cells of domain d, then -1 in the remaining slots; every row has 32 or more cells, and all rows of some domain are full. `neighbours`: an entry is -1, another local cell of the same domain, or 1024 + j * 128 + p for a ghost slot p that the sending domain fills; slot 0 of every cell is valid. `drag_coef`: Positive. `kernel`: positive and symmetric.
All inputs are finite; a program needn't handle non-finite values.
Results may differ from the reference program's by a relative error of at most 0.0048.
Values may be sent and summed in bfloat16 or wider, within the bound.
A program may use at most 64 MiB of HBM per device.

```python
import math
import jax
import jax.numpy as jnp
from jax import lax

NB = 128
FACES = 8
CELL_DEV = 1024
GH = 128
DOMS = 64
CELLS = 65536


OFFSETS = (1, -1, 2, -2)


def ghost_counts(key):
    base = jax.random.fold_in(key, 11)
    counts = jax.random.randint(jax.random.fold_in(base, 1), (DOMS, 4), GH // 4, GH + 1, dtype=jnp.int32)
    chosen = jax.random.randint(jax.random.fold_in(base, 2), (), 0, DOMS, dtype=jnp.int32)
    domain_rows = jnp.arange(DOMS, dtype=jnp.int32)[:, None]
    return jnp.where(domain_rows == chosen, GH, counts).astype(jnp.int32)


def draw_send_cells(key, part):
    counts = ghost_counts(key)
    keys = jax.random.split(jax.random.fold_in(key, 12), DOMS * 4)
    picked = jax.vmap(lambda single: jax.random.permutation(single, CELL_DEV)[:GH])(keys)
    picked = picked.reshape(DOMS, 4, GH).astype(jnp.int32)
    slots = jnp.arange(GH, dtype=jnp.int32)[None, None, :]
    return jnp.where(slots < counts[:, :, None], picked, -1).astype(jnp.int32)


def draw_neighbours(key, part):
    counts = ghost_counts(key)
    base = jax.random.fold_in(key, 13)
    shape = (FACES, DOMS, CELL_DEV)
    kind = jax.random.randint(jax.random.fold_in(base, 1), shape, 0, 4, dtype=jnp.int32)
    kind = kind.at[0].set(1)
    local_cell = jnp.arange(CELL_DEV, dtype=jnp.int32)[None, None, :]
    stride = jax.random.randint(jax.random.fold_in(base, 2), shape, 1, CELL_DEV, dtype=jnp.int32)
    local_pick = (local_cell + stride) % CELL_DEV
    block = jax.random.randint(jax.random.fold_in(base, 3), shape, 0, 4, dtype=jnp.int32)
    domain = jnp.arange(DOMS, dtype=jnp.int32)[None, :, None]
    offsets = jnp.array(OFFSETS, jnp.int32)
    source = (domain - offsets[block]) % DOMS
    avail = counts[source, block]
    slot = jax.random.randint(jax.random.fold_in(base, 4), shape, 0, avail, dtype=jnp.int32)
    ghost_pick = CELL_DEV + block * GH + slot
    result = jnp.where(kind == 1, local_pick, jnp.where(kind >= 2, ghost_pick, -1))
    forced = CELL_DEV + 3 * GH + counts[(jnp.arange(DOMS, dtype=jnp.int32) + 2) % DOMS, 3] - 1
    result = result.at[FACES - 1, :, 0].set(forced)
    return result.reshape(FACES, DOMS * CELL_DEV).astype(jnp.int32)


def draw_drag_coef(key, part):
    ranks = jnp.arange(NB, dtype=jnp.float32) / NB
    factor = jnp.exp(jax.random.uniform(key, (NB,), jnp.float32, -0.35, 0.35))
    return (jnp.exp(2.302585 * (4.0 * ranks - 3.0)) * factor).astype(jnp.float32)


def draw_kernel(key, part):
    base = jax.random.fold_in(key, 21)
    strong_pair = jax.random.randint(base, (NB, NB), 0, 4, dtype=jnp.int32) < 1
    upper_half = jnp.arange(NB, dtype=jnp.int32)[:, None] <= jnp.arange(NB, dtype=jnp.int32)[None, :]
    strong_pair = jnp.where(upper_half, strong_pair, strong_pair.T)
    return jnp.where(strong_pair, 0.0703125, 0.001953125).astype(jnp.bfloat16)


def levels(rng, shape, cuts, least, largest):
    level = 1.0
    for position, parts in cuts:
        heights = jax.random.uniform(jax.random.fold_in(jax.random.fold_in(rng, 6), position), (parts,), jnp.float32, least / len(cuts), largest / len(cuts))
        level = level * jnp.repeat(jnp.exp(heights), shape[position] // parts).reshape((-1,) + (1,) * (len(shape) - 1 - position))
    return level


def noise(rng, extent, width, limit, cuts=(), held_as=jnp.bfloat16):
    values = jax.random.normal(rng, extent, jnp.float32) * width
    if len(cuts) > 0:
        values = levels(rng, extent, cuts, -0.22, 0.18) * values
    return jnp.clip(values, min=-limit, max=limit).astype(held_as)


def setup_inputs(seed: int = 0) -> dict:
    key_list = jax.random.split(jax.random.key(seed), 13)
    return {
        "dust_rho": jnp.clip(jnp.exp(math.log(4.0) - 2.7725887 * jax.random.uniform(key_list[0], (NB, CELLS), jnp.float32) ** levels(key_list[0], (NB, CELLS), ((0, 8), (1, 64)), -0.2, 0.2)), 0.25, 4.0),
        "dust_vel": noise(key_list[1], (2, NB, CELLS), 1.0, 4.0, ((1, 8), (2, 64)), jnp.float32),
        "gas_rho": jnp.clip(jnp.exp(math.log(500.0) - 2.3025851 * jax.random.uniform(key_list[2], (CELLS,), jnp.float32) ** levels(key_list[2], (CELLS,), ((0, 64),), -0.2, 0.2)), 50.0, 500.0),
        "gas_vel": noise(key_list[3], (2, CELLS), 1.0, 4.0, ((1, 64),), jnp.float32),
        "normals": noise(key_list[4], (2, FACES, CELLS), 0.08, 0.24, ((2, 64),), jnp.float32),
        "inv_volume": jnp.clip(jnp.exp(math.log(3.0) - 1.3862944 * jax.random.uniform(key_list[5], (CELLS,), jnp.float32) ** levels(key_list[5], (CELLS,), ((0, 64),), -0.2, 0.2)), 0.75, 3.0),
        "coag_rate": jnp.clip(jnp.exp(math.log(0.3) - 2.3025852 * jax.random.uniform(key_list[6], (CELLS,), jnp.float32) ** levels(key_list[6], (CELLS,), ((0, 64),), -0.2, 0.2)), 0.03, 0.3),
        "drag_coef": draw_drag_coef(jax.random.fold_in(key_list[12], 71), 0),
        "neighbours": draw_neighbours(jax.random.fold_in(key_list[12], 71), 0),
        "send_cells": draw_send_cells(jax.random.fold_in(key_list[12], 71), 0),
        "kernel": draw_kernel(jax.random.fold_in(key_list[12], 71), 0),
        "redistrib": noise(key_list[11], (NB, NB), NB ** -0.5, 0.5),
    }


OFFSETS = (1, -1, 2, -2)


def minmod(first, second):
    return 0.5 * (jnp.sign(first) + jnp.sign(second)) * jnp.minimum(jnp.abs(first), jnp.abs(second))


def advect(state, extended, faces, face_normals, inv_vol):
    density = state[0]
    vel_x = state[1]
    vel_y = state[2]
    total_mean = jnp.zeros_like(density)
    valid_count = jnp.zeros(density.shape[1:], jnp.float32)
    saved = []
    for face in range(faces.shape[0]):
        index = faces[face]
        valid = index >= 0
        safe = jnp.where(valid, index, 0)
        other = jnp.take(extended[0], safe, axis=1)
        saved.append(other)
        total_mean = total_mean + jnp.where(valid, other, 0.0)
        valid_count = valid_count + valid.astype(jnp.float32)
    neighbour_mean = total_mean / valid_count
    flux_total = jnp.zeros_like(density)
    for face in range(faces.shape[0]):
        index = faces[face]
        valid = index >= 0
        safe = jnp.where(valid, index, 0)
        others = jnp.take(extended[1:], safe, axis=2)
        other = saved[face]
        speed = 0.5 * ((vel_x + others[0]) * face_normals[0, face] + (vel_y + others[1]) * face_normals[1, face])
        limited = minmod(other - density, density - neighbour_mean)
        flux = jnp.maximum(speed, 0.0) * (density + 0.5 * limited) + jnp.minimum(speed, 0.0) * (other - 0.5 * limited)
        flux_total = flux_total + jnp.where(valid, flux, 0.0)
    return density - inv_vol * flux_total


def reference(dust_rho, dust_vel, gas_rho, gas_vel, normals, inv_volume, coag_rate, drag_coef, neighbours, send_cells, kernel, redistrib):
    coupling = drag_coef[:, None] * gas_rho[None, :]
    share = coupling / (1.0 + coupling)
    weight = dust_rho / gas_rho[None, :] * share
    sum_zero = jnp.sum(weight, axis=0)
    sum_x = jnp.sum(weight * dust_vel[0], axis=0)
    sum_y = jnp.sum(weight * dust_vel[1], axis=0)
    gas_vel_out = (gas_vel + jnp.stack([sum_x, sum_y])) / (1.0 + sum_zero)
    dust_vel_out = (dust_vel + coupling[None] * gas_vel_out[:, None, :]) / (1.0 + coupling[None])
    state = jnp.concatenate([dust_rho[None], dust_vel_out], axis=0)

    def one_domain(domain):
        start = (domain * CELL_DEV).astype(jnp.int32)
        own = lax.dynamic_slice_in_dim(state, start, CELL_DEV, 2)
        blocks = [own]
        for direction in range(4):
            source = ((domain - OFFSETS[direction]) % DOMS).astype(jnp.int32)
            index = send_cells[source, direction]
            source_state = lax.dynamic_slice_in_dim(state, (source * CELL_DEV).astype(jnp.int32), CELL_DEV, 2)
            picked = jnp.take(source_state, jnp.maximum(index, 0), axis=2)
            blocks.append(picked * (index >= 0).astype(jnp.float32))
        extended = jnp.concatenate(blocks, axis=2)
        faces = lax.dynamic_slice_in_dim(neighbours, start, CELL_DEV, 1)
        face_normals = lax.dynamic_slice_in_dim(normals, start, CELL_DEV, 2)
        inv_vol = lax.dynamic_slice_in_dim(inv_volume, start, CELL_DEV, 0)
        return advect(own, extended, faces, face_normals, inv_vol)

    moved_blocks = lax.map(one_domain, jnp.arange(DOMS, dtype=jnp.int32))
    moved = jnp.transpose(moved_blocks, (1, 0, 2)).reshape(NB, DOMS * CELL_DEV)
    rounded = moved.astype(jnp.bfloat16)
    collide = jnp.dot(kernel, rounded, preferred_element_type=jnp.float32)
    loss = (coag_rate[None, :] * rounded.astype(jnp.float32) * collide).astype(jnp.bfloat16)
    gain = jnp.dot(redistrib, loss, preferred_element_type=jnp.float32)
    dust_rho_out = moved - loss.astype(jnp.float32) + gain
    return dust_rho_out, dust_vel_out, gas_vel_out
```

```python
import jax
import jax.numpy as jnp
from jax import lax
from jax.experimental import pallas as pl
from jax.experimental.pallas import tpu as pltpu
from jax.sharding import PartitionSpec as P

OFFSETS = (1, -1, 2, -2)
LANES = 128
SUB = 8
MESH = pl.DeviceIdType.MESH


def spread(row):
    return jnp.broadcast_to(row, (SUB, LANES))


def lane_take(block, lanes):
    return jnp.take_along_axis(block, lanes, axis=1, mode="promise_in_bounds")


def minmod(first, second):
    return jnp.maximum(jnp.minimum(first, second), 0.0) + jnp.minimum(
        jnp.maximum(first, second), 0.0
    )


def kernel_body(
    bins,
    doms,
    rho_ref,
    vel_ref,
    gas_rho_ref,
    gas_vel_ref,
    normals_ref,
    inv_ref,
    coag_ref,
    drag_ref,
    faces_ref,
    send_ref,
    kern_ref,
    redis_ref,
    rho_out,
    vel_out,
    gas_out,
    ext,
    picked,
    sums,
    ghost_out,
    moved,
    rounded,
    mixed,
    delta,
    back,
    sum_send,
    sum_recv,
    rho_send,
    rho_recv,
    vel_send,
    vel_recv,
    mix_send,
    mix_recv,
    back_send,
    back_recv,
):
    rows = rho_ref.shape[0]
    groups = rho_ref.shape[1] // LANES
    face_count = faces_ref.shape[0]
    halves = rows // SUB
    me = lax.axis_index("bin")
    dom = lax.axis_index("dom")

    barrier = pltpu.get_barrier_semaphore()
    for step in range(1, bins):
        pl.semaphore_signal(
            barrier, inc=1, device_id={"bin": lax.rem(me + step, bins)}, device_id_type=MESH
        )
    for offset in OFFSETS:
        pl.semaphore_signal(
            barrier,
            inc=1,
            device_id={"dom": lax.rem(dom + offset + doms, doms)},
            device_id_type=MESH,
        )

    diagonal = lax.broadcasted_iota(jnp.int32, (rows, rows), 0) == lax.broadcasted_iota(
        jnp.int32, (rows, rows), 1
    )
    drag = jnp.sum(
        jnp.where(diagonal, jnp.broadcast_to(drag_ref[...], (rows, rows)), 0.0),
        axis=1,
        keepdims=True,
    )

    for c in range(groups):
        cells = slice(c * LANES, (c + 1) * LANES)
        density = rho_ref[:, cells]
        ext[c, 0:rows, :] = density
        gas_rho = gas_rho_ref[c : c + 1, :]
        coupling = drag * gas_rho
        weight = density / gas_rho * (coupling / (1.0 + coupling))
        sums[me, 0, c : c + 1, :] = jnp.sum(weight, axis=0, keepdims=True)
        sums[me, 1, c : c + 1, :] = jnp.sum(weight * vel_ref[0, :, cells], axis=0, keepdims=True)
        sums[me, 2, c : c + 1, :] = jnp.sum(weight * vel_ref[1, :, cells], axis=0, keepdims=True)

    def choose(first_row, last_row):
        for j in range(len(OFFSETS)):
            index = spread(send_ref[j : j + 1, :])
            safe = jnp.maximum(index, 0)
            lanes = safe & (LANES - 1)
            block = safe >> 7
            for r in range(first_row, last_row, SUB):
                value = lane_take(ext[0, r : r + SUB, :], lanes)
                for s in range(1, groups):
                    value = jnp.where(
                        block == s, lane_take(ext[s, r : r + SUB, :], lanes), value
                    )
                ghost_out[j, r : r + SUB, :] = jnp.where(index >= 0, value, 0.0)

    def ghost_copy(j, first_row, last_row, send_sem, recv_sem):
        return pltpu.make_async_remote_copy(
            src_ref=ghost_out.at[j, first_row:last_row],
            dst_ref=ext.at[groups + j, first_row:last_row],
            send_sem=send_sem.at[j],
            recv_sem=recv_sem.at[j],
            device_id={"dom": lax.rem(dom + OFFSETS[j] + doms, doms)},
            device_id_type=MESH,
        )

    choose(0, rows)
    pl.semaphore_wait(barrier, bins - 1 + len(OFFSETS))

    def peer_copy(step, source, target, send_sem, recv_sem):
        return pltpu.make_async_remote_copy(
            src_ref=source,
            dst_ref=target,
            send_sem=send_sem.at[step],
            recv_sem=recv_sem.at[step],
            device_id={"bin": lax.rem(me + step, bins)},
            device_id_type=MESH,
        )

    def peer_arrived(step, source, buffer, send_sem, recv_sem):
        sender = lax.rem(me + bins - step, bins)
        peer_copy(step, source, buffer.at[sender], send_sem, recv_sem).wait_recv()

    for step in range(1, bins):
        peer_copy(step, sums.at[me], sums.at[me], sum_send, sum_recv).start()
    for j in range(len(OFFSETS)):
        ghost_copy(j, 0, rows, rho_send, rho_recv).start()

    def pick(first_block, last_block, first_row, last_row):
        def group(c, carry):
            cells = pl.ds(pl.multiple_of(c * LANES, LANES), LANES)
            for k in range(face_count):
                safe = jnp.maximum(spread(faces_ref[k : k + 1, cells]), 0)
                lanes = safe & (LANES - 1)
                block = safe >> 7
                for r in range(first_row, last_row, SUB):
                    if first_block == 0:
                        value = lane_take(ext[0, r : r + SUB, :], lanes)
                    else:
                        value = picked[c, k, r : r + SUB, :]
                    for s in range(max(first_block, 1), last_block):
                        value = jnp.where(
                            block == s, lane_take(ext[s, r : r + SUB, :], lanes), value
                        )
                    picked[c, k, r : r + SUB, :] = value
            return carry

        lax.fori_loop(0, groups, group, 0)

    total_blocks = groups + len(OFFSETS)
    pick(0, groups, 0, rows)
    for j in range(len(OFFSETS)):
        ghost_copy(j, 0, rows, rho_send, rho_recv).wait_recv()
    pick(groups, total_blocks, 0, rows)

    for step in range(1, bins):
        peer_arrived(step, sums.at[me], sums, sum_send, sum_recv)
    totals = sums[0]
    for b in range(1, bins):
        totals = totals + sums[b]

    for c in range(groups):
        cells = slice(c * LANES, (c + 1) * LANES)
        scale = 1.0 + totals[0, c : c + 1, :]
        coupling = drag * gas_rho_ref[c : c + 1, :]
        for component in range(2):
            gas = (
                gas_vel_ref[component : component + 1, cells]
                + totals[component + 1, c : c + 1, :]
            ) / scale
            gas_out[component : component + 1, cells] = gas
            dust = (vel_ref[component, :, cells] + coupling * gas) / (1.0 + coupling)
            vel_out[component, :, cells] = dust
            ext[c, (component + 1) * rows : (component + 2) * rows, :] = dust

    choose(rows, 3 * rows)
    for j in range(len(OFFSETS)):
        ghost_copy(j, rows, 3 * rows, vel_send, vel_recv).start()
    pick(0, groups, rows, 3 * rows)
    for j in range(len(OFFSETS)):
        ghost_copy(j, rows, 3 * rows, vel_send, vel_recv).wait_recv()
    pick(groups, total_blocks, rows, 3 * rows)

    def advect(c, carry):
        cells = pl.ds(pl.multiple_of(c * LANES, LANES), LANES)
        valid = [spread(faces_ref[k : k + 1, cells]) >= 0 for k in range(face_count)]
        count = valid[0].astype(jnp.float32)
        for k in range(1, face_count):
            count = count + valid[k].astype(jnp.float32)
        inverse = spread(inv_ref[pl.ds(c, 1), :])
        for h in range(halves):
            first = slice(h * SUB, (h + 1) * SUB)
            second = slice(rows + h * SUB, rows + (h + 1) * SUB)
            third = slice(2 * rows + h * SUB, 2 * rows + (h + 1) * SUB)
            density = ext[c, first, :]
            vel_x = ext[c, second, :]
            vel_y = ext[c, third, :]
            mean = jnp.where(valid[0], picked[c, 0, first, :], 0.0)
            for k in range(1, face_count):
                mean = mean + jnp.where(valid[k], picked[c, k, first, :], 0.0)
            slope = density - mean / count
            total = jnp.zeros((SUB, LANES), jnp.float32)
            for k in range(face_count):
                other = picked[c, k, first, :]
                speed = 0.5 * (
                    (vel_x + picked[c, k, second, :]) * spread(normals_ref[0, k : k + 1, cells])
                    + (vel_y + picked[c, k, third, :]) * spread(normals_ref[1, k : k + 1, cells])
                )
                limited = 0.5 * minmod(other - density, slope)
                flux = jnp.maximum(speed, 0.0) * (density + limited) + jnp.minimum(speed, 0.0) * (
                    other - limited
                )
                total = total + jnp.where(valid[k], flux, 0.0)
            moved[c, first, :] = density - inverse * total
        rounded[c] = moved[c].astype(jnp.bfloat16)
        return carry

    lax.fori_loop(0, groups, advect, 0)

    for step in range(1, bins):
        peer = lax.rem(me + step, bins)
        peer_copy(step, rounded.at[peer], mixed.at[me], mix_send, mix_recv).start()
    mixed[me] = rounded[me]
    for step in range(1, bins):
        peer_arrived(step, rounded.at[0], mixed, mix_send, mix_recv)
    columns = mixed[...].reshape(bins * rows, LANES)
    collide = jnp.dot(kern_ref[...], columns, preferred_element_type=jnp.float32)
    rate = coag_ref[pl.ds(me, 1), :]
    loss = (rate * columns.astype(jnp.float32) * collide).astype(jnp.bfloat16)
    gain = jnp.dot(redis_ref[...], loss, preferred_element_type=jnp.float32)
    delta[...] = (gain - loss.astype(jnp.float32)).reshape(bins, rows, LANES)
    for step in range(1, bins):
        peer = lax.rem(me + step, bins)
        peer_copy(step, delta.at[peer], back.at[me], back_send, back_recv).start()
    back[me] = delta[me]
    for step in range(1, bins):
        peer_arrived(step, delta.at[0], back, back_send, back_recv)
    for c in range(groups):
        rho_out[:, c * LANES : (c + 1) * LANES] = moved[c] + back[c]

    for step in range(1, bins):
        peer = lax.rem(me + step, bins)
        peer_copy(step, sums.at[me], sums.at[me], sum_send, sum_recv).wait_send()
        peer_copy(step, rounded.at[peer], mixed.at[me], mix_send, mix_recv).wait_send()
        peer_copy(step, delta.at[peer], back.at[me], back_send, back_recv).wait_send()
    for j in range(len(OFFSETS)):
        ghost_copy(j, 0, rows, rho_send, rho_recv).wait_send()
        ghost_copy(j, rows, 3 * rows, vel_send, vel_recv).wait_send()


def body(
    dust_rho,
    dust_vel,
    gas_rho,
    gas_vel,
    normals,
    inv_volume,
    coag_rate,
    drag_coef,
    neighbours,
    send_cells,
    kernel,
    redistrib,
):
    rows, cells = dust_rho.shape
    bins = lax.axis_size("bin")
    doms = lax.axis_size("dom")
    groups = cells // LANES
    faces = neighbours.shape[0]
    ghosts = len(OFFSETS)

    def run(*refs):
        kernel_body(bins, doms, *refs)

    vmem = pl.BlockSpec(memory_space=pltpu.VMEM)
    dma = pltpu.SemaphoreType.DMA
    return pl.pallas_call(
        run,
        name="dust_step",
        out_shape=(
            jax.ShapeDtypeStruct(dust_rho.shape, jnp.float32),
            jax.ShapeDtypeStruct(dust_vel.shape, jnp.float32),
            jax.ShapeDtypeStruct(gas_vel.shape, jnp.float32),
        ),
        in_specs=[vmem] * 12,
        out_specs=(vmem, vmem, vmem),
        scratch_shapes=[
            pltpu.VMEM((groups + ghosts, 3 * rows, LANES), jnp.float32),
            pltpu.VMEM((groups, faces, 3 * rows, LANES), jnp.float32),
            pltpu.VMEM((bins, 3, groups, LANES), jnp.float32),
            pltpu.VMEM((ghosts, 3 * rows, LANES), jnp.float32),
            pltpu.VMEM((groups, rows, LANES), jnp.float32),
            pltpu.VMEM((groups, rows, LANES), jnp.bfloat16),
            pltpu.VMEM((bins, rows, LANES), jnp.bfloat16),
            pltpu.VMEM((bins, rows, LANES), jnp.float32),
            pltpu.VMEM((bins, rows, LANES), jnp.float32),
            dma((bins,)),
            dma((bins,)),
            dma((ghosts,)),
            dma((ghosts,)),
            dma((ghosts,)),
            dma((ghosts,)),
            dma((bins,)),
            dma((bins,)),
            dma((bins,)),
            dma((bins,)),
        ],
        compiler_params=pltpu.CompilerParams(collective_id=0, has_side_effects=True),
    )(
        dust_rho,
        dust_vel,
        gas_rho.reshape(groups, LANES),
        gas_vel,
        normals,
        inv_volume.reshape(groups, LANES),
        coag_rate.reshape(groups, LANES),
        drag_coef.reshape(1, rows),
        neighbours,
        send_cells.reshape(ghosts, LANES),
        kernel,
        redistrib,
    )


def solution(mesh):
    placed = (
        P("bin", "dom"),
        P(None, "bin", "dom"),
        P("dom"),
        P(None, "dom"),
        P(None, None, "dom"),
        P("dom"),
        P("dom"),
        P("bin"),
        P(None, "dom"),
        P("dom", None, None),
        P(),
        P(),
    )
    return jax.shard_map(
        body,
        mesh=mesh,
        in_specs=placed,
        out_specs=(P("bin", "dom"), P(None, "bin", "dom"), P(None, "dom")),
        check_vma=False,
    )
```

```python
import jax
import jax.numpy as jnp
from jax import lax
from jax.experimental import pallas as pl
from jax.experimental.pallas import tpu as pltpu
from jax.sharding import PartitionSpec as P

OFFSETS = (1, -1, 2, -2)
LANES = 128
SUB = 8
MESH = pl.DeviceIdType.MESH
STEPS = 8191.0
MIDDLE = 32768.0
UNROLL = 4


def spread(row):
    return jnp.broadcast_to(row, (SUB, LANES))


def lane_take(block, lanes):
    return jnp.take_along_axis(block, lanes, axis=1, mode="promise_in_bounds")


def join(vel_x, vel_y):
    first = (vel_x * STEPS + (MIDDLE + 0.5)).astype(jnp.int32)
    second = (vel_y * STEPS + (MIDDLE + 0.5)).astype(jnp.int32)
    return first * 65536 + second


def minmod(first, second):
    return jnp.maximum(jnp.minimum(first, second), 0.0) + jnp.minimum(
        jnp.maximum(first, second), 0.0
    )


def kernel_body(
    bins,
    doms,
    *refs,
):
    held = refs[:12]
    rho_out, vel_out, gas_out = refs[12:15]
    inputs = refs[15:27]
    loaded = refs[27]
    (
        rho_ref,
        vel_ref,
        gas_rho_ref,
        gas_vel_ref,
        normals_ref,
        inv_ref,
        coag_ref,
        drag_ref,
        faces_ref,
        send_ref,
        kern_ref,
        redis_ref,
    ) = inputs
    (
        ext,
        coded,
        picked,
        picked_vel,
        sums,
        ghost_out,
        moved,
        rounded,
        mixed,
        delta,
        back,
        sum_send,
        sum_recv,
        rho_send,
        rho_recv,
        vel_send,
        vel_recv,
        mix_send,
        mix_recv,
        back_send,
        back_recv,
    ) = refs[28:]
    rows = rho_ref.shape[0]
    groups = rho_ref.shape[1] // LANES
    face_count = faces_ref.shape[0]
    halves = rows // SUB
    me = lax.axis_index("bin")
    dom = lax.axis_index("dom")

    barrier = pltpu.get_barrier_semaphore()
    for step in range(1, bins):
        pl.semaphore_signal(
            barrier, inc=1, device_id={"bin": lax.rem(me + step, bins)}, device_id_type=MESH
        )
    for offset in OFFSETS:
        pl.semaphore_signal(
            barrier,
            inc=1,
            device_id={"dom": lax.rem(dom + offset + doms, doms)},
            device_id_type=MESH,
        )

    loads = [
        pltpu.make_async_copy(held[i], inputs[i], loaded.at[i]) for i in range(len(inputs))
    ]
    for i in (0, 2, 7, 9, 1, 8, 3, 4, 5, 6, 10, 11):
        loads[i].start()
    for i in (0, 2, 7, 1):
        loads[i].wait()

    diagonal = lax.broadcasted_iota(jnp.int32, (rows, rows), 0) == lax.broadcasted_iota(
        jnp.int32, (rows, rows), 1
    )
    drag = jnp.sum(
        jnp.where(diagonal, jnp.broadcast_to(drag_ref[...], (rows, rows)), 0.0),
        axis=1,
        keepdims=True,
    )

    for c in range(groups):
        cells = slice(c * LANES, (c + 1) * LANES)
        density = rho_ref[:, cells]
        ext[c, 0:rows, :] = density
        gas_rho = gas_rho_ref[c : c + 1, :]
        coupling = drag * gas_rho
        weight = density / gas_rho * (coupling / (1.0 + coupling))
        sums[me, 0, c : c + 1, :] = jnp.sum(weight, axis=0, keepdims=True)
        sums[me, 1, c : c + 1, :] = jnp.sum(weight * vel_ref[0, :, cells], axis=0, keepdims=True)
        sums[me, 2, c : c + 1, :] = jnp.sum(weight * vel_ref[1, :, cells], axis=0, keepdims=True)

    def choose(first_row, last_row):
        for j in range(len(OFFSETS)):
            index = spread(send_ref[j : j + 1, :])
            safe = jnp.maximum(index, 0)
            lanes = safe & (LANES - 1)
            block = safe >> 7
            for r in range(first_row, last_row, SUB):
                value = lane_take(ext[0, r : r + SUB, :], lanes)
                for s in range(1, groups):
                    value = jnp.where(
                        block == s, lane_take(ext[s, r : r + SUB, :], lanes), value
                    )
                ghost_out[j, r : r + SUB, :] = jnp.where(index >= 0, value, 0.0)

    def ghost_copy(j, first_row, last_row, send_sem, recv_sem):
        return pltpu.make_async_remote_copy(
            src_ref=ghost_out.at[j, first_row:last_row],
            dst_ref=ext.at[groups + j, first_row:last_row],
            send_sem=send_sem.at[j],
            recv_sem=recv_sem.at[j],
            device_id={"dom": lax.rem(dom + OFFSETS[j] + doms, doms)},
            device_id_type=MESH,
        )

    loads[9].wait()
    choose(0, rows)
    pl.semaphore_wait(barrier, bins - 1 + len(OFFSETS))

    def peer_copy(step, source, target, send_sem, recv_sem):
        return pltpu.make_async_remote_copy(
            src_ref=source,
            dst_ref=target,
            send_sem=send_sem.at[step],
            recv_sem=recv_sem.at[step],
            device_id={"bin": lax.rem(me + step, bins)},
            device_id_type=MESH,
        )

    def peer_arrived(step, source, buffer, send_sem, recv_sem):
        sender = lax.rem(me + bins - step, bins)
        peer_copy(step, source, buffer.at[sender], send_sem, recv_sem).wait_recv()

    for step in range(1, bins):
        peer_copy(step, sums.at[me], sums.at[me], sum_send, sum_recv).start()
    for j in range(len(OFFSETS)):
        ghost_copy(j, 0, rows, rho_send, rho_recv).start()

    def pick(first_block, last_block, source, target, c, faces):
        cells = pl.ds(pl.multiple_of(c * LANES, LANES), LANES)
        for k in faces:
            safe = jnp.maximum(spread(faces_ref[k : k + 1, cells]), 0)
            lanes = safe & (LANES - 1)
            block = safe >> 7
            for r in range(0, rows, SUB):
                if first_block == 0:
                    value = lane_take(source[0, r : r + SUB, :], lanes)
                else:
                    value = target[c, k, r : r + SUB, :]
                for s in range(max(first_block, 1), last_block):
                    value = jnp.where(
                        block == s, lane_take(source[s, r : r + SUB, :], lanes), value
                    )
                target[c, k, r : r + SUB, :] = value

    def pick_all(first_block, last_block, source, target):
        def part(i, carry):
            for u in range(UNROLL):
                pick(first_block, last_block, source, target, i * UNROLL + u, range(face_count))
            return carry

        lax.fori_loop(0, groups // UNROLL, part, 0)

    total_blocks = groups + len(OFFSETS)
    loads[8].wait()
    pick_all(0, groups, ext, picked)
    for j in range(len(OFFSETS)):
        ghost_copy(j, 0, rows, rho_send, rho_recv).wait_recv()
    pick_all(groups, total_blocks, ext, picked)
    for i in (3, 4, 5, 6, 10, 11):
        loads[i].wait()

    for step in range(1, bins):
        peer_arrived(step, sums.at[me], sums, sum_send, sum_recv)
    totals = sums[0]
    for b in range(1, bins):
        totals = totals + sums[b]

    for c in range(groups):
        cells = slice(c * LANES, (c + 1) * LANES)
        scale = 1.0 + totals[0, c : c + 1, :]
        coupling = drag * gas_rho_ref[c : c + 1, :]
        both = []
        for component in range(2):
            gas = (
                gas_vel_ref[component : component + 1, cells]
                + totals[component + 1, c : c + 1, :]
            ) / scale
            gas_out[component : component + 1, cells] = gas
            dust = (vel_ref[component, :, cells] + coupling * gas) / (1.0 + coupling)
            vel_out[component, :, cells] = dust
            ext[c, (component + 1) * rows : (component + 2) * rows, :] = dust
            both.append(dust)
        coded[c] = join(both[0], both[1])

    choose(rows, 3 * rows)
    for j in range(len(OFFSETS)):
        ghost_copy(j, rows, 3 * rows, vel_send, vel_recv).start()
    pick_all(0, groups, coded, picked_vel)
    for j in range(len(OFFSETS)):
        ghost_copy(j, rows, 3 * rows, vel_send, vel_recv).wait_recv()
        coded[groups + j] = join(
            ext[groups + j, rows : 2 * rows, :], ext[groups + j, 2 * rows : 3 * rows, :]
        )

    def advect(c):
        pick(groups, total_blocks, coded, picked_vel, c, range(face_count))
        cells = pl.ds(pl.multiple_of(c * LANES, LANES), LANES)
        valid = [spread(faces_ref[k : k + 1, cells]) >= 0 for k in range(face_count)]
        count = valid[0].astype(jnp.float32)
        for k in range(1, face_count):
            count = count + valid[k].astype(jnp.float32)
        inverse = spread(inv_ref[pl.ds(c, 1), :])
        for h in range(halves):
            first = slice(h * SUB, (h + 1) * SUB)
            second = slice(rows + h * SUB, rows + (h + 1) * SUB)
            third = slice(2 * rows + h * SUB, 2 * rows + (h + 1) * SUB)
            density = ext[c, first, :]
            vel_x = ext[c, second, :] - MIDDLE / STEPS
            vel_y = ext[c, third, :] - MIDDLE / STEPS
            mean = jnp.where(valid[0], picked[c, 0, first, :], 0.0)
            for k in range(1, face_count):
                mean = mean + jnp.where(valid[k], picked[c, k, first, :], 0.0)
            slope = density - mean / count
            total = jnp.zeros((SUB, LANES), jnp.float32)
            for k in range(face_count):
                other = picked[c, k, first, :]
                pair = picked_vel[c, k, first, :]
                other_x = lax.shift_right_logical(pair, 16).astype(jnp.float32) * (1.0 / STEPS)
                other_y = (pair & 65535).astype(jnp.float32) * (1.0 / STEPS)
                speed = 0.5 * (
                    (vel_x + other_x) * spread(normals_ref[0, k : k + 1, cells])
                    + (vel_y + other_y) * spread(normals_ref[1, k : k + 1, cells])
                )
                limited = 0.5 * minmod(other - density, slope)
                flux = jnp.maximum(speed, 0.0) * (density + limited) + jnp.minimum(speed, 0.0) * (
                    other - limited
                )
                total = total + jnp.where(valid[k], flux, 0.0)
            moved[c, first, :] = density - inverse * total
        rounded[c] = moved[c].astype(jnp.bfloat16)

    order = [(bins // 2 + turn) % bins for turn in (0, 1, 7, 3, 2, 5, 6, 4)]
    for first in range(0, bins, UNROLL):
        for step in order[first : first + UNROLL]:
            advect(lax.rem(me + step, bins))
        for step in order[first : first + UNROLL]:
            if step > 0:
                peer = lax.rem(me + step, bins)
                peer_copy(step, rounded.at[peer], mixed.at[me], mix_send, mix_recv).start()
    mixed[me] = rounded[me]
    for step in range(1, bins):
        peer_arrived(step, rounded.at[0], mixed, mix_send, mix_recv)
    columns = mixed[...].reshape(bins * rows, LANES)
    collide = jnp.dot(kern_ref[...], columns, preferred_element_type=jnp.float32)
    rate = coag_ref[pl.ds(me, 1), :]
    loss = (rate * columns.astype(jnp.float32) * collide).astype(jnp.bfloat16)
    gain = jnp.dot(redis_ref[...], loss, preferred_element_type=jnp.float32)
    delta[...] = (gain - loss.astype(jnp.float32)).reshape(bins, rows, LANES)
    for step in range(1, bins):
        peer = lax.rem(me + step, bins)
        peer_copy(step, delta.at[peer], back.at[me], back_send, back_recv).start()
    back[me] = delta[me]
    for step in range(1, bins):
        peer_arrived(step, delta.at[0], back, back_send, back_recv)
    for c in range(groups):
        rho_out[:, c * LANES : (c + 1) * LANES] = moved[c] + back[c]

    for step in range(1, bins):
        peer = lax.rem(me + step, bins)
        peer_copy(step, sums.at[me], sums.at[me], sum_send, sum_recv).wait_send()
        peer_copy(step, rounded.at[peer], mixed.at[me], mix_send, mix_recv).wait_send()
        peer_copy(step, delta.at[peer], back.at[me], back_send, back_recv).wait_send()
    for j in range(len(OFFSETS)):
        ghost_copy(j, 0, rows, rho_send, rho_recv).wait_send()
        ghost_copy(j, rows, 3 * rows, vel_send, vel_recv).wait_send()


def body(
    dust_rho,
    dust_vel,
    gas_rho,
    gas_vel,
    normals,
    inv_volume,
    coag_rate,
    drag_coef,
    neighbours,
    send_cells,
    kernel,
    redistrib,
):
    rows, cells = dust_rho.shape
    bins = lax.axis_size("bin")
    doms = lax.axis_size("dom")
    groups = cells // LANES
    faces = neighbours.shape[0]
    ghosts = len(OFFSETS)

    def run(*refs):
        kernel_body(bins, doms, *refs)

    arrays = (
        dust_rho,
        dust_vel,
        gas_rho.reshape(groups, LANES),
        gas_vel,
        normals,
        inv_volume.reshape(groups, LANES),
        coag_rate.reshape(groups, LANES),
        drag_coef.reshape(1, rows),
        neighbours,
        send_cells.reshape(ghosts, LANES),
        kernel,
        redistrib,
    )
    vmem = pl.BlockSpec(memory_space=pltpu.VMEM)
    dma = pltpu.SemaphoreType.DMA
    return pl.pallas_call(
        run,
        name="dust_step",
        out_shape=(
            jax.ShapeDtypeStruct(dust_rho.shape, jnp.float32),
            jax.ShapeDtypeStruct(dust_vel.shape, jnp.float32),
            jax.ShapeDtypeStruct(gas_vel.shape, jnp.float32),
        ),
        in_specs=[pl.BlockSpec(memory_space=pl.ANY)] * len(arrays),
        out_specs=(vmem, vmem, vmem),
        scratch_shapes=[pltpu.VMEM(array.shape, array.dtype) for array in arrays]
        + [
            dma((len(arrays),)),
            pltpu.VMEM((groups + ghosts, 3 * rows, LANES), jnp.float32),
            pltpu.VMEM((groups + ghosts, rows, LANES), jnp.int32),
            pltpu.VMEM((groups, faces, rows, LANES), jnp.float32),
            pltpu.VMEM((groups, faces, rows, LANES), jnp.int32),
            pltpu.VMEM((bins, 3, groups, LANES), jnp.float32),
            pltpu.VMEM((ghosts, 3 * rows, LANES), jnp.float32),
            pltpu.VMEM((groups, rows, LANES), jnp.float32),
            pltpu.VMEM((groups, rows, LANES), jnp.bfloat16),
            pltpu.VMEM((bins, rows, LANES), jnp.bfloat16),
            pltpu.VMEM((bins, rows, LANES), jnp.float32),
            pltpu.VMEM((bins, rows, LANES), jnp.float32),
            dma((bins,)),
            dma((bins,)),
            dma((ghosts,)),
            dma((ghosts,)),
            dma((ghosts,)),
            dma((ghosts,)),
            dma((bins,)),
            dma((bins,)),
            dma((bins,)),
            dma((bins,)),
        ],
        compiler_params=pltpu.CompilerParams(collective_id=0, has_side_effects=True),
    )(*arrays)


def solution(mesh):
    placed = (
        P("bin", "dom"),
        P(None, "bin", "dom"),
        P("dom"),
        P(None, "dom"),
        P(None, None, "dom"),
        P("dom"),
        P("dom"),
        P("bin"),
        P(None, "dom"),
        P("dom", None, None),
        P(),
        P(),
    )
    return jax.shard_map(
        body,
        mesh=mesh,
        in_specs=placed,
        out_specs=(P("bin", "dom"), P(None, "bin", "dom"), P(None, "dom")),
        check_vma=False,
    )
```

```python
import jax
import jax.numpy as jnp
from jax import lax
from jax.experimental import pallas as pl
from jax.experimental.pallas import tpu as pltpu
from jax.sharding import PartitionSpec as P

OFFSETS = (1, -1, 2, -2)
LANES = 128
SUB = 8
MESH = pl.DeviceIdType.MESH
STEPS = 8191.0
MIDDLE = 32768.0
UNROLL = 4


def spread(row):
    return jnp.broadcast_to(row, (SUB, LANES))


def lane_take(block, lanes):
    return jnp.take_along_axis(block, lanes, axis=1, mode="promise_in_bounds")


def join(vel_x, vel_y):
    first = (vel_x * STEPS + (MIDDLE + 0.5)).astype(jnp.int32)
    second = (vel_y * STEPS + (MIDDLE + 0.5)).astype(jnp.int32)
    return first * 65536 + second


def minmod(first, second):
    return jnp.maximum(jnp.minimum(first, second), 0.0) + jnp.minimum(
        jnp.maximum(first, second), 0.0
    )


def kernel_body(
    bins,
    doms,
    *refs,
):
    held = refs[:12]
    rho_out, vel_out, gas_out = refs[12:15]
    inputs = refs[15:27]
    loaded = refs[27]
    (
        rho_ref,
        vel_ref,
        gas_rho_ref,
        gas_vel_ref,
        normals_ref,
        inv_ref,
        coag_ref,
        drag_ref,
        faces_ref,
        send_ref,
        kern_ref,
        redis_ref,
    ) = inputs
    (
        ext,
        coded,
        picked,
        picked_vel,
        sums,
        ghost_out,
        moved,
        rounded,
        mixed,
        delta,
        back,
        sum_send,
        sum_recv,
        rho_send,
        rho_recv,
        vel_send,
        vel_recv,
        mix_send,
        mix_recv,
        back_send,
        back_recv,
    ) = refs[28:]
    rows = rho_ref.shape[0]
    groups = rho_ref.shape[1] // LANES
    face_count = faces_ref.shape[0]
    halves = rows // SUB
    me = lax.axis_index("bin")
    dom = lax.axis_index("dom")

    barrier = pltpu.get_barrier_semaphore()
    for step in range(1, bins):
        pl.semaphore_signal(
            barrier, inc=1, device_id={"bin": lax.rem(me + step, bins)}, device_id_type=MESH
        )
    for offset in OFFSETS:
        pl.semaphore_signal(
            barrier,
            inc=1,
            device_id={"dom": lax.rem(dom + offset + doms, doms)},
            device_id_type=MESH,
        )

    loads = [
        pltpu.make_async_copy(held[i], inputs[i], loaded.at[i]) for i in range(len(inputs))
    ]
    for i in (0, 2, 7, 9, 1, 8, 3, 4, 5, 6, 10, 11):
        loads[i].start()
    for i in (0, 2, 7, 1):
        loads[i].wait()

    diagonal = lax.broadcasted_iota(jnp.int32, (rows, rows), 0) == lax.broadcasted_iota(
        jnp.int32, (rows, rows), 1
    )
    drag = jnp.sum(
        jnp.where(diagonal, jnp.broadcast_to(drag_ref[...], (rows, rows)), 0.0),
        axis=1,
        keepdims=True,
    )

    for c in range(groups):
        cells = slice(c * LANES, (c + 1) * LANES)
        density = rho_ref[:, cells]
        ext[c, 0:rows, :] = density
        gas_rho = gas_rho_ref[c : c + 1, :]
        coupling = drag * gas_rho
        weight = density / gas_rho * (coupling / (1.0 + coupling))
        sums[me, 0, c : c + 1, :] = jnp.sum(weight, axis=0, keepdims=True)
        sums[me, 1, c : c + 1, :] = jnp.sum(weight * vel_ref[0, :, cells], axis=0, keepdims=True)
        sums[me, 2, c : c + 1, :] = jnp.sum(weight * vel_ref[1, :, cells], axis=0, keepdims=True)

    def choose(first_row, last_row):
        for j in range(len(OFFSETS)):
            index = spread(send_ref[j : j + 1, :])
            safe = jnp.maximum(index, 0)
            lanes = safe & (LANES - 1)
            block = safe >> 7
            for r in range(first_row, last_row, SUB):
                value = lane_take(ext[0, r : r + SUB, :], lanes)
                for s in range(1, groups):
                    value = jnp.where(
                        block == s, lane_take(ext[s, r : r + SUB, :], lanes), value
                    )
                ghost_out[j, r : r + SUB, :] = jnp.where(index >= 0, value, 0.0)

    def ghost_copy(j, first_row, last_row, send_sem, recv_sem):
        return pltpu.make_async_remote_copy(
            src_ref=ghost_out.at[j, first_row:last_row],
            dst_ref=ext.at[groups + j, first_row:last_row],
            send_sem=send_sem.at[j],
            recv_sem=recv_sem.at[j],
            device_id={"dom": lax.rem(dom + OFFSETS[j] + doms, doms)},
            device_id_type=MESH,
        )

    loads[9].wait()
    choose(0, rows)
    pl.semaphore_wait(barrier, bins - 1 + len(OFFSETS))

    def peer_copy(step, source, target, send_sem, recv_sem):
        return pltpu.make_async_remote_copy(
            src_ref=source,
            dst_ref=target,
            send_sem=send_sem.at[step],
            recv_sem=recv_sem.at[step],
            device_id={"bin": lax.rem(me + step, bins)},
            device_id_type=MESH,
        )

    def peer_arrived(step, source, buffer, send_sem, recv_sem):
        sender = lax.rem(me + bins - step, bins)
        peer_copy(step, source, buffer.at[sender], send_sem, recv_sem).wait_recv()

    for step in range(1, bins):
        peer_copy(step, sums.at[me], sums.at[me], sum_send, sum_recv).start()
    for j in range(len(OFFSETS)):
        ghost_copy(j, 0, rows, rho_send, rho_recv).start()

    def pick(first_block, last_block, source, target, c, faces):
        cells = pl.ds(pl.multiple_of(c * LANES, LANES), LANES)
        for k in faces:
            safe = jnp.maximum(spread(faces_ref[k : k + 1, cells]), 0)
            lanes = safe & (LANES - 1)
            block = safe >> 7
            for r in range(0, rows, SUB):
                if first_block == 0:
                    value = lane_take(source[0, r : r + SUB, :], lanes)
                else:
                    value = target[c, k, r : r + SUB, :]
                for s in range(max(first_block, 1), last_block):
                    value = jnp.where(
                        block == s, lane_take(source[s, r : r + SUB, :], lanes), value
                    )
                target[c, k, r : r + SUB, :] = value

    def pick_all(first_block, last_block, source, target):
        def part(i, carry):
            for u in range(UNROLL):
                pick(first_block, last_block, source, target, i * UNROLL + u, range(face_count))
            return carry

        lax.fori_loop(0, groups // UNROLL, part, 0)

    total_blocks = groups + len(OFFSETS)
    loads[8].wait()
    pick_all(0, groups, ext, picked)
    for j in range(len(OFFSETS)):
        ghost_copy(j, 0, rows, rho_send, rho_recv).wait_recv()
    pick_all(groups, total_blocks, ext, picked)
    for i in (3, 4, 5, 6, 10, 11):
        loads[i].wait()

    for step in range(1, bins):
        peer_arrived(step, sums.at[me], sums, sum_send, sum_recv)
    totals = sums[0]
    for b in range(1, bins):
        totals = totals + sums[b]

    for c in range(groups):
        cells = slice(c * LANES, (c + 1) * LANES)
        scale = 1.0 + totals[0, c : c + 1, :]
        coupling = drag * gas_rho_ref[c : c + 1, :]
        both = []
        for component in range(2):
            gas = (
                gas_vel_ref[component : component + 1, cells]
                + totals[component + 1, c : c + 1, :]
            ) / scale
            gas_out[component : component + 1, cells] = gas
            dust = (vel_ref[component, :, cells] + coupling * gas) / (1.0 + coupling)
            vel_out[component, :, cells] = dust
            ext[c, (component + 1) * rows : (component + 2) * rows, :] = dust
            both.append(dust)
        coded[c] = join(both[0], both[1])

    choose(rows, 3 * rows)
    for j in range(len(OFFSETS)):
        ghost_copy(j, rows, 3 * rows, vel_send, vel_recv).start()
    pick_all(0, groups, coded, picked_vel)
    for j in range(len(OFFSETS)):
        ghost_copy(j, rows, 3 * rows, vel_send, vel_recv).wait_recv()
        coded[groups + j] = join(
            ext[groups + j, rows : 2 * rows, :], ext[groups + j, 2 * rows : 3 * rows, :]
        )

    def advect(c):
        pick(groups, total_blocks, coded, picked_vel, c, range(face_count))
        cells = pl.ds(pl.multiple_of(c * LANES, LANES), LANES)
        valid = [spread(faces_ref[k : k + 1, cells]) >= 0 for k in range(face_count)]
        count = valid[0].astype(jnp.float32)
        for k in range(1, face_count):
            count = count + valid[k].astype(jnp.float32)
        inverse = spread(inv_ref[pl.ds(c, 1), :])
        for h in range(halves):
            first = slice(h * SUB, (h + 1) * SUB)
            second = slice(rows + h * SUB, rows + (h + 1) * SUB)
            third = slice(2 * rows + h * SUB, 2 * rows + (h + 1) * SUB)
            density = ext[c, first, :]
            vel_x = ext[c, second, :] - MIDDLE / STEPS
            vel_y = ext[c, third, :] - MIDDLE / STEPS
            mean = jnp.where(valid[0], picked[c, 0, first, :], 0.0)
            for k in range(1, face_count):
                mean = mean + jnp.where(valid[k], picked[c, k, first, :], 0.0)
            slope = density - mean / count
            total = jnp.zeros((SUB, LANES), jnp.float32)
            for k in range(face_count):
                other = picked[c, k, first, :]
                pair = picked_vel[c, k, first, :]
                other_x = lax.shift_right_logical(pair, 16).astype(jnp.float32) * (1.0 / STEPS)
                other_y = (pair & 65535).astype(jnp.float32) * (1.0 / STEPS)
                speed = 0.5 * (
                    (vel_x + other_x) * spread(normals_ref[0, k : k + 1, cells])
                    + (vel_y + other_y) * spread(normals_ref[1, k : k + 1, cells])
                )
                limited = 0.5 * minmod(other - density, slope)
                flux = jnp.maximum(speed, 0.0) * (density + limited) + jnp.minimum(speed, 0.0) * (
                    other - limited
                )
                total = total + jnp.where(valid[k], flux, 0.0)
            moved[c, first, :] = density - inverse * total
        rounded[c] = moved[c].astype(jnp.bfloat16)

    order = [(bins // 2 + turn) % bins for turn in (0, 1, 7, 3, 2, 5, 6, 4)]
    for first in range(0, bins, UNROLL):
        for step in order[first : first + UNROLL]:
            advect(lax.rem(me + step, bins))
        for step in order[first : first + UNROLL]:
            if step > 0:
                peer = lax.rem(me + step, bins)
                peer_copy(step, rounded.at[peer], mixed.at[me], mix_send, mix_recv).start()
    mixed[me] = rounded[me]
    for step in range(1, bins):
        peer_arrived(step, rounded.at[0], mixed, mix_send, mix_recv)
    columns = mixed[...].reshape(bins * rows, LANES)
    collide = jnp.dot(kern_ref[...], columns, preferred_element_type=jnp.float32)
    rate = coag_ref[pl.ds(me, 1), :]
    loss = (rate * columns.astype(jnp.float32) * collide).astype(jnp.bfloat16)
    gain = jnp.dot(redis_ref[...], loss, preferred_element_type=jnp.float32)
    delta[...] = (gain - loss.astype(jnp.float32)).reshape(bins, rows, LANES)
    for step in range(1, bins):
        peer = lax.rem(me + step, bins)
        peer_copy(step, delta.at[peer], back.at[me], back_send, back_recv).start()
    back[me] = delta[me]
    for step in range(1, bins):
        peer_arrived(step, delta.at[0], back, back_send, back_recv)
    for c in range(groups):
        rho_out[:, c * LANES : (c + 1) * LANES] = moved[c] + back[c]

    for step in range(1, bins):
        peer = lax.rem(me + step, bins)
        peer_copy(step, sums.at[me], sums.at[me], sum_send, sum_recv).wait_send()
        peer_copy(step, rounded.at[peer], mixed.at[me], mix_send, mix_recv).wait_send()
        peer_copy(step, delta.at[peer], back.at[me], back_send, back_recv).wait_send()
    for j in range(len(OFFSETS)):
        ghost_copy(j, 0, rows, rho_send, rho_recv).wait_send()
        ghost_copy(j, rows, 3 * rows, vel_send, vel_recv).wait_send()


def store_body(rho, vel, gas, rho_out, vel_out, gas_out, stored):
    pairs = ((rho, rho_out), (vel, vel_out), (gas, gas_out))
    copies = [
        pltpu.make_async_copy(source, target, stored.at[i])
        for i, (source, target) in enumerate(pairs)
    ]
    for copy in copies:
        copy.start()
    for copy in copies:
        copy.wait()


def body(
    dust_rho,
    dust_vel,
    gas_rho,
    gas_vel,
    normals,
    inv_volume,
    coag_rate,
    drag_coef,
    neighbours,
    send_cells,
    kernel,
    redistrib,
):
    rows, cells = dust_rho.shape
    bins = lax.axis_size("bin")
    doms = lax.axis_size("dom")
    groups = cells // LANES
    faces = neighbours.shape[0]
    ghosts = len(OFFSETS)

    def run(*refs):
        kernel_body(bins, doms, *refs)

    arrays = (
        dust_rho,
        dust_vel,
        gas_rho.reshape(groups, LANES),
        gas_vel,
        normals,
        inv_volume.reshape(groups, LANES),
        coag_rate.reshape(groups, LANES),
        drag_coef.reshape(1, rows),
        neighbours,
        send_cells.reshape(ghosts, LANES),
        kernel,
        redistrib,
    )
    shapes = (dust_rho.shape, dust_vel.shape, gas_vel.shape)
    vmem = pl.BlockSpec(memory_space=pltpu.VMEM)
    dma = pltpu.SemaphoreType.DMA
    results = pl.pallas_call(
        run,
        name="dust_step",
        out_shape=tuple(pltpu.VMEM(shape, jnp.float32) for shape in shapes),
        in_specs=[pl.BlockSpec(memory_space=pl.ANY)] * len(arrays),
        out_specs=(vmem, vmem, vmem),
        scratch_shapes=[pltpu.VMEM(array.shape, array.dtype) for array in arrays]
        + [
            dma((len(arrays),)),
            pltpu.VMEM((groups + ghosts, 3 * rows, LANES), jnp.float32),
            pltpu.VMEM((groups + ghosts, rows, LANES), jnp.int32),
            pltpu.VMEM((groups, faces, rows, LANES), jnp.float32),
            pltpu.VMEM((groups, faces, rows, LANES), jnp.int32),
            pltpu.VMEM((bins, 3, groups, LANES), jnp.float32),
            pltpu.VMEM((ghosts, 3 * rows, LANES), jnp.float32),
            pltpu.VMEM((groups, rows, LANES), jnp.float32),
            pltpu.VMEM((groups, rows, LANES), jnp.bfloat16),
            pltpu.VMEM((bins, rows, LANES), jnp.bfloat16),
            pltpu.VMEM((bins, rows, LANES), jnp.float32),
            pltpu.VMEM((bins, rows, LANES), jnp.float32),
            dma((bins,)),
            dma((bins,)),
            dma((ghosts,)),
            dma((ghosts,)),
            dma((ghosts,)),
            dma((ghosts,)),
            dma((bins,)),
            dma((bins,)),
            dma((bins,)),
            dma((bins,)),
        ],
        compiler_params=pltpu.CompilerParams(collective_id=0, has_side_effects=True),
    )(*arrays)
    return pl.pallas_call(
        store_body,
        name="dust_store",
        out_shape=tuple(jax.ShapeDtypeStruct(shape, jnp.float32) for shape in shapes),
        in_specs=[vmem] * 3,
        out_specs=(pl.BlockSpec(memory_space=pl.ANY),) * 3,
        scratch_shapes=[dma((3,))],
        compiler_params=pltpu.CompilerParams(vmem_limit_bytes=1 << 20),
    )(*results)


def solution(mesh):
    placed = (
        P("bin", "dom"),
        P(None, "bin", "dom"),
        P("dom"),
        P(None, "dom"),
        P(None, None, "dom"),
        P("dom"),
        P("dom"),
        P("bin"),
        P(None, "dom"),
        P("dom", None, None),
        P(),
        P(),
    )
    return jax.shard_map(
        body,
        mesh=mesh,
        in_specs=placed,
        out_specs=(P("bin", "dom"), P(None, "bin", "dom"), P(None, "dom")),
        check_vma=False,
    )
```

```python
import jax
import jax.numpy as jnp
from jax import lax
from jax.experimental import pallas as pl
from jax.experimental.pallas import tpu as pltpu
from jax.sharding import PartitionSpec as P

OFFSETS = (1, -1, 2, -2)
LANES = 128
SUB = 8
MESH = pl.DeviceIdType.MESH
STEPS = 8191.0
MIDDLE = 32768.0
UNROLL = 4


def spread(row):
    return jnp.broadcast_to(row, (SUB, LANES))


def lane_take(block, lanes):
    return jnp.take_along_axis(block, lanes, axis=1, mode="promise_in_bounds")


def join(vel_x, vel_y):
    first = (vel_x * STEPS + (MIDDLE + 0.5)).astype(jnp.int32)
    second = (vel_y * STEPS + (MIDDLE + 0.5)).astype(jnp.int32)
    return first * 65536 + second


def minmod(first, second):
    return jnp.maximum(jnp.minimum(first, second), 0.0) + jnp.minimum(
        jnp.maximum(first, second), 0.0
    )


def kernel_body(
    bins,
    doms,
    *refs,
):
    held = refs[:12]
    rho_out, vel_out, gas_out = refs[12:15]
    inputs = refs[15:27]
    loaded = refs[27]
    (
        rho_ref,
        vel_ref,
        gas_rho_ref,
        gas_vel_ref,
        normals_ref,
        inv_ref,
        coag_ref,
        drag_ref,
        faces_ref,
        send_ref,
        kern_ref,
        redis_ref,
    ) = inputs
    (
        ext,
        coded,
        picked,
        picked_vel,
        partial,
        sums,
        gas_held,
        fixed,
        share_held,
        ghost_rho,
        ghost_vel,
        ghost_in,
        moved,
        rounded,
        mixed,
        delta,
        back,
        sum_send,
        sum_recv,
        rho_send,
        rho_recv,
        vel_send,
        vel_recv,
        mix_send,
        mix_recv,
        back_send,
        back_recv,
    ) = refs[28:]
    rows = rho_ref.shape[0]
    groups = rho_ref.shape[1] // LANES
    face_count = faces_ref.shape[0]
    halves = rows // SUB
    me = lax.axis_index("bin")
    dom = lax.axis_index("dom")

    barrier = pltpu.get_barrier_semaphore()
    for step in range(1, bins):
        pl.semaphore_signal(
            barrier, inc=1, device_id={"bin": lax.rem(me + step, bins)}, device_id_type=MESH
        )
    for offset in OFFSETS:
        pl.semaphore_signal(
            barrier,
            inc=1,
            device_id={"dom": lax.rem(dom + offset + doms, doms)},
            device_id_type=MESH,
        )

    loads = [
        pltpu.make_async_copy(held[i], inputs[i], loaded.at[i]) for i in range(len(inputs))
    ]
    for i in (0, 2, 7, 9, 1, 8, 3, 4, 5, 6, 10, 11):
        loads[i].start()
    for i in (0, 2, 7, 1):
        loads[i].wait()

    diagonal = lax.broadcasted_iota(jnp.int32, (rows, rows), 0) == lax.broadcasted_iota(
        jnp.int32, (rows, rows), 1
    )
    drag = jnp.sum(
        jnp.where(diagonal, jnp.broadcast_to(drag_ref[...], (rows, rows)), 0.0),
        axis=1,
        keepdims=True,
    )

    for c in range(groups):
        cells = slice(c * LANES, (c + 1) * LANES)
        density = rho_ref[:, cells]
        ext[c, 0:rows, :] = density
        gas_rho = gas_rho_ref[c : c + 1, :]
        coupling = drag * gas_rho
        weight = density / gas_rho * (coupling / (1.0 + coupling))
        partial[0, c : c + 1, :] = jnp.sum(weight, axis=0, keepdims=True)
        partial[1, c : c + 1, :] = jnp.sum(weight * vel_ref[0, :, cells], axis=0, keepdims=True)
        partial[2, c : c + 1, :] = jnp.sum(weight * vel_ref[1, :, cells], axis=0, keepdims=True)
    sums[me] = partial[...].astype(jnp.bfloat16)

    def choose(first_row, target):
        for j in range(len(OFFSETS)):
            index = spread(send_ref[j : j + 1, :])
            safe = jnp.maximum(index, 0)
            lanes = safe & (LANES - 1)
            block = safe >> 7
            parts = []
            for r in range(first_row, first_row + target.shape[1], SUB):
                value = lane_take(ext[0, r : r + SUB, :], lanes)
                for s in range(1, groups):
                    value = jnp.where(
                        block == s, lane_take(ext[s, r : r + SUB, :], lanes), value
                    )
                parts.append(jnp.where(index >= 0, value, 0.0))
            target[j] = jnp.concatenate(parts, axis=0).astype(target.dtype)

    def ghost_copy(j, source, target, send_sem, recv_sem):
        return pltpu.make_async_remote_copy(
            src_ref=source,
            dst_ref=target,
            send_sem=send_sem.at[j],
            recv_sem=recv_sem.at[j],
            device_id={"dom": lax.rem(dom + OFFSETS[j] + doms, doms)},
            device_id_type=MESH,
        )

    def rho_copy(j):
        target = ext.at[groups + j, 0:rows]
        return ghost_copy(j, ghost_rho.at[j], target, rho_send, rho_recv)

    def vel_copy(j):
        return ghost_copy(j, ghost_vel.at[j], ghost_in.at[j], vel_send, vel_recv)

    loads[9].wait()
    choose(0, ghost_rho)
    pl.semaphore_wait(barrier, bins - 1 + len(OFFSETS))

    def peer_copy(step, source, target, send_sem, recv_sem):
        return pltpu.make_async_remote_copy(
            src_ref=source,
            dst_ref=target,
            send_sem=send_sem.at[step],
            recv_sem=recv_sem.at[step],
            device_id={"bin": lax.rem(me + step, bins)},
            device_id_type=MESH,
        )

    def peer_arrived(step, source, buffer, send_sem, recv_sem):
        sender = lax.rem(me + bins - step, bins)
        peer_copy(step, source, buffer.at[sender], send_sem, recv_sem).wait_recv()

    order = [(bins // 2 + turn) % bins for turn in (0, 1, 7, 3, 2, 5, 6, 4)]
    for step in order[:-1]:
        peer_copy(step, sums.at[me], sums.at[me], sum_send, sum_recv).start()
    for j in range(len(OFFSETS)):
        rho_copy(j).start()
    loads[3].wait()
    for c in range(groups):
        cells = slice(c * LANES, (c + 1) * LANES)
        coupling = drag * gas_rho_ref[c : c + 1, :]
        inverse = 1.0 / (1.0 + coupling)
        share_held[c] = coupling / (1.0 + coupling)
        for component in range(2):
            fixed[component, c] = vel_ref[component, :, cells] * inverse
            gas_held[component, c : c + 1, :] = gas_vel_ref[component : component + 1, cells]

    def pick(first_block, last_block, source, target, c, faces):
        cells = pl.ds(pl.multiple_of(c * LANES, LANES), LANES)
        for k in faces:
            safe = jnp.maximum(spread(faces_ref[k : k + 1, cells]), 0)
            lanes = safe & (LANES - 1)
            block = safe >> 7
            for r in range(0, rows, SUB):
                if first_block == 0:
                    value = lane_take(source[0, r : r + SUB, :], lanes)
                else:
                    value = target[c, k, r : r + SUB, :]
                for s in range(max(first_block, 1), last_block):
                    value = jnp.where(
                        block == s, lane_take(source[s, r : r + SUB, :], lanes), value
                    )
                target[c, k, r : r + SUB, :] = value

    def pick_all(first_block, last_block, source, target):
        def part(i, carry):
            for u in range(UNROLL):
                pick(first_block, last_block, source, target, i * UNROLL + u, range(face_count))
            return carry

        lax.fori_loop(0, groups // UNROLL, part, 0)

    total_blocks = groups + len(OFFSETS)
    loads[8].wait()
    pick_all(0, groups, ext, picked)
    for j in range(len(OFFSETS)):
        rho_copy(j).wait_recv()
    pick_all(groups, total_blocks, ext, picked)
    for i in (4, 5, 6, 10, 11):
        loads[i].wait()

    for step in range(1, bins):
        peer_arrived(step, sums.at[me], sums, sum_send, sum_recv)
    totals = sums[0].astype(jnp.float32)
    for b in range(1, bins):
        totals = totals + sums[b].astype(jnp.float32)
    gas_held[...] = (gas_held[...] + totals[1:]) / (1.0 + totals[0:1])
    for c in range(groups):
        cells = slice(c * LANES, (c + 1) * LANES)
        share = share_held[c]
        both = []
        for component in range(2):
            gas = gas_held[component, c : c + 1, :]
            gas_out[component : component + 1, cells] = gas
            dust = fixed[component, c] + share * gas
            vel_out[component, :, cells] = dust
            ext[c, (component + 1) * rows : (component + 2) * rows, :] = dust
            both.append(dust)
        coded[c] = join(both[0], both[1])

    choose(rows, ghost_vel)
    for j in range(len(OFFSETS)):
        vel_copy(j).start()
    pick_all(0, groups, coded, picked_vel)
    for j in range(len(OFFSETS)):
        vel_copy(j).wait_recv()
        coded[groups + j] = join(
            ghost_in[j, 0:rows].astype(jnp.float32),
            ghost_in[j, rows : 2 * rows].astype(jnp.float32),
        )

    def advect(c):
        pick(groups, total_blocks, coded, picked_vel, c, range(face_count))
        cells = pl.ds(pl.multiple_of(c * LANES, LANES), LANES)
        valid = [spread(faces_ref[k : k + 1, cells]) >= 0 for k in range(face_count)]
        count = valid[0].astype(jnp.float32)
        for k in range(1, face_count):
            count = count + valid[k].astype(jnp.float32)
        inverse = spread(inv_ref[pl.ds(c, 1), :])
        for h in range(halves):
            first = slice(h * SUB, (h + 1) * SUB)
            second = slice(rows + h * SUB, rows + (h + 1) * SUB)
            third = slice(2 * rows + h * SUB, 2 * rows + (h + 1) * SUB)
            density = ext[c, first, :]
            vel_x = ext[c, second, :] - MIDDLE / STEPS
            vel_y = ext[c, third, :] - MIDDLE / STEPS
            mean = jnp.where(valid[0], picked[c, 0, first, :], 0.0)
            for k in range(1, face_count):
                mean = mean + jnp.where(valid[k], picked[c, k, first, :], 0.0)
            slope = density - mean / count
            total = jnp.zeros((SUB, LANES), jnp.float32)
            for k in range(face_count):
                other = picked[c, k, first, :]
                pair = picked_vel[c, k, first, :]
                other_x = lax.shift_right_logical(pair, 16).astype(jnp.float32) * (1.0 / STEPS)
                other_y = (pair & 65535).astype(jnp.float32) * (1.0 / STEPS)
                speed = 0.5 * (
                    (vel_x + other_x) * spread(normals_ref[0, k : k + 1, cells])
                    + (vel_y + other_y) * spread(normals_ref[1, k : k + 1, cells])
                )
                limited = 0.5 * minmod(other - density, slope)
                flux = jnp.maximum(speed, 0.0) * (density + limited) + jnp.minimum(speed, 0.0) * (
                    other - limited
                )
                total = total + jnp.where(valid[k], flux, 0.0)
            moved[c, first, :] = density - inverse * total
        rounded[c] = moved[c].astype(jnp.bfloat16)

    for first in range(0, bins, UNROLL):
        for step in order[first : first + UNROLL]:
            advect(lax.rem(me + step, bins))
        for step in order[first : first + UNROLL]:
            if step > 0:
                peer = lax.rem(me + step, bins)
                peer_copy(step, rounded.at[peer], mixed.at[me], mix_send, mix_recv).start()
    mixed[me] = rounded[me]
    for step in range(1, bins):
        peer_arrived(step, rounded.at[0], mixed, mix_send, mix_recv)
    columns = mixed[...].reshape(bins * rows, LANES)
    collide = jnp.dot(kern_ref[...], columns, preferred_element_type=jnp.float32)
    rate = coag_ref[pl.ds(me, 1), :]
    loss = (rate * columns.astype(jnp.float32) * collide).astype(jnp.bfloat16)
    gain = jnp.dot(redis_ref[...], loss, preferred_element_type=jnp.float32)
    change = gain - loss.astype(jnp.float32)
    delta[...] = change.astype(jnp.bfloat16).reshape(bins, rows, LANES)
    for step in order[:-1]:
        peer = lax.rem(me + step, bins)
        peer_copy(step, delta.at[peer], back.at[me], back_send, back_recv).start()
    back[me] = delta[me]
    for step in range(1, bins):
        peer_arrived(step, delta.at[0], back, back_send, back_recv)
    for c in range(groups):
        rho_out[:, c * LANES : (c + 1) * LANES] = moved[c] + back[c].astype(jnp.float32)

    for step in range(1, bins):
        peer = lax.rem(me + step, bins)
        peer_copy(step, sums.at[me], sums.at[me], sum_send, sum_recv).wait_send()
        peer_copy(step, rounded.at[peer], mixed.at[me], mix_send, mix_recv).wait_send()
        peer_copy(step, delta.at[peer], back.at[me], back_send, back_recv).wait_send()
    for j in range(len(OFFSETS)):
        rho_copy(j).wait_send()
        vel_copy(j).wait_send()


def store_body(rho, vel, gas, rho_out, vel_out, gas_out, stored):
    pairs = ((rho, rho_out), (vel, vel_out), (gas, gas_out))
    copies = [
        pltpu.make_async_copy(source, target, stored.at[i])
        for i, (source, target) in enumerate(pairs)
    ]
    for copy in copies:
        copy.start()
    for copy in copies:
        copy.wait()


def body(
    dust_rho,
    dust_vel,
    gas_rho,
    gas_vel,
    normals,
    inv_volume,
    coag_rate,
    drag_coef,
    neighbours,
    send_cells,
    kernel,
    redistrib,
):
    rows, cells = dust_rho.shape
    bins = lax.axis_size("bin")
    doms = lax.axis_size("dom")
    groups = cells // LANES
    faces = neighbours.shape[0]
    ghosts = len(OFFSETS)

    def run(*refs):
        kernel_body(bins, doms, *refs)

    arrays = (
        dust_rho,
        dust_vel,
        gas_rho.reshape(groups, LANES),
        gas_vel,
        normals,
        inv_volume.reshape(groups, LANES),
        coag_rate.reshape(groups, LANES),
        drag_coef.reshape(1, rows),
        neighbours,
        send_cells.reshape(ghosts, LANES),
        kernel,
        redistrib,
    )
    shapes = (dust_rho.shape, dust_vel.shape, gas_vel.shape)
    vmem = pl.BlockSpec(memory_space=pltpu.VMEM)
    dma = pltpu.SemaphoreType.DMA
    results = pl.pallas_call(
        run,
        name="dust_step",
        out_shape=tuple(pltpu.VMEM(shape, jnp.float32) for shape in shapes),
        in_specs=[pl.BlockSpec(memory_space=pl.ANY)] * len(arrays),
        out_specs=(vmem, vmem, vmem),
        scratch_shapes=[pltpu.VMEM(array.shape, array.dtype) for array in arrays]
        + [
            dma((len(arrays),)),
            pltpu.VMEM((groups + ghosts, 3 * rows, LANES), jnp.float32),
            pltpu.VMEM((groups + ghosts, rows, LANES), jnp.int32),
            pltpu.VMEM((groups, faces, rows, LANES), jnp.float32),
            pltpu.VMEM((groups, faces, rows, LANES), jnp.int32),
            pltpu.VMEM((3, groups, LANES), jnp.float32),
            pltpu.VMEM((bins, 3, groups, LANES), jnp.bfloat16),
            pltpu.VMEM((2, groups, LANES), jnp.float32),
            pltpu.VMEM((2, groups, rows, LANES), jnp.float32),
            pltpu.VMEM((groups, rows, LANES), jnp.float32),
            pltpu.VMEM((ghosts, rows, LANES), jnp.float32),
            pltpu.VMEM((ghosts, 2 * rows, LANES), jnp.bfloat16),
            pltpu.VMEM((ghosts, 2 * rows, LANES), jnp.bfloat16),
            pltpu.VMEM((groups, rows, LANES), jnp.float32),
            pltpu.VMEM((groups, rows, LANES), jnp.bfloat16),
            pltpu.VMEM((bins, rows, LANES), jnp.bfloat16),
            pltpu.VMEM((bins, rows, LANES), jnp.bfloat16),
            pltpu.VMEM((bins, rows, LANES), jnp.bfloat16),
            dma((bins,)),
            dma((bins,)),
            dma((ghosts,)),
            dma((ghosts,)),
            dma((ghosts,)),
            dma((ghosts,)),
            dma((bins,)),
            dma((bins,)),
            dma((bins,)),
            dma((bins,)),
        ],
        compiler_params=pltpu.CompilerParams(collective_id=0, has_side_effects=True),
    )(*arrays)
    return pl.pallas_call(
        store_body,
        name="dust_store",
        out_shape=tuple(jax.ShapeDtypeStruct(shape, jnp.float32) for shape in shapes),
        in_specs=[vmem] * 3,
        out_specs=(pl.BlockSpec(memory_space=pl.ANY),) * 3,
        scratch_shapes=[dma((3,))],
        compiler_params=pltpu.CompilerParams(vmem_limit_bytes=1 << 20),
    )(*results)


def solution(mesh):
    placed = (
        P("bin", "dom"),
        P(None, "bin", "dom"),
        P("dom"),
        P(None, "dom"),
        P(None, None, "dom"),
        P("dom"),
        P("dom"),
        P("bin"),
        P(None, "dom"),
        P("dom", None, None),
        P(),
        P(),
    )
    return jax.shard_map(
        body,
        mesh=mesh,
        in_specs=placed,
        out_specs=(P("bin", "dom"), P(None, "bin", "dom"), P(None, "dom")),
        check_vma=False,
    )
```

```python
import jax
import jax.numpy as jnp
from jax import lax
from jax.experimental import pallas as pl
from jax.experimental.pallas import tpu as pltpu
from jax.sharding import PartitionSpec as P

OFFSETS = (1, -1, 2, -2)
LANES = 128
SUB = 8
MESH = pl.DeviceIdType.MESH
STEPS = 8191.0
MIDDLE = 32768.0
UNROLL = 4


def spread(row):
    return jnp.broadcast_to(row, (SUB, LANES))


def lane_take(block, lanes):
    return jnp.take_along_axis(block, lanes, axis=1, mode="promise_in_bounds")


def join(vel_x, vel_y):
    first = (vel_x * STEPS + (MIDDLE + 0.5)).astype(jnp.int32)
    second = (vel_y * STEPS + (MIDDLE + 0.5)).astype(jnp.int32)
    return first * 65536 + second


def minmod(first, second):
    return jnp.maximum(jnp.minimum(first, second), 0.0) + jnp.minimum(
        jnp.maximum(first, second), 0.0
    )


def kernel_body(
    bins,
    doms,
    *refs,
):
    held = refs[:12]
    rho_out, vel_out, gas_out = refs[12:15]
    inputs = refs[15:27]
    loaded = refs[27]
    (
        rho_ref,
        vel_ref,
        gas_rho_ref,
        gas_vel_ref,
        normals_ref,
        inv_ref,
        coag_ref,
        drag_ref,
        faces_ref,
        send_ref,
        kern_ref,
        redis_ref,
    ) = inputs
    (
        ext,
        coded,
        picked,
        picked_vel,
        after,
        partial,
        sums,
        ghost_partial,
        ghost_sums,
        gas_held,
        fixed,
        share_held,
        ghost_rho,
        ghost_vel,
        ghost_in,
        moved,
        rounded,
        mixed,
        delta,
        back,
        sum_send,
        sum_recv,
        add_send,
        add_recv,
        rho_send,
        rho_recv,
        vel_send,
        vel_recv,
        mix_send,
        mix_recv,
        back_send,
        back_recv,
    ) = refs[28:]
    rows = rho_ref.shape[0]
    groups = rho_ref.shape[1] // LANES
    face_count = faces_ref.shape[0]
    halves = rows // SUB
    me = lax.axis_index("bin")
    dom = lax.axis_index("dom")

    barrier = pltpu.get_barrier_semaphore()
    for step in range(1, bins):
        pl.semaphore_signal(
            barrier, inc=1, device_id={"bin": lax.rem(me + step, bins)}, device_id_type=MESH
        )
    for offset in OFFSETS:
        pl.semaphore_signal(
            barrier,
            inc=1,
            device_id={"dom": lax.rem(dom + offset + doms, doms)},
            device_id_type=MESH,
        )

    loads = [
        pltpu.make_async_copy(held[i], inputs[i], loaded.at[i]) for i in range(len(inputs))
    ]
    for i in (0, 2, 7, 1, 3, 9, 8, 4, 5, 6, 10, 11):
        loads[i].start()
    for i in (0, 2, 7, 1, 3):
        loads[i].wait()

    diagonal = lax.broadcasted_iota(jnp.int32, (rows, rows), 0) == lax.broadcasted_iota(
        jnp.int32, (rows, rows), 1
    )
    drag = jnp.sum(
        jnp.where(diagonal, jnp.broadcast_to(drag_ref[...], (rows, rows)), 0.0),
        axis=1,
        keepdims=True,
    )

    for c in range(groups):
        cells = slice(c * LANES, (c + 1) * LANES)
        density = rho_ref[:, cells]
        ext[c, 0:rows, :] = density
        gas_rho = gas_rho_ref[c : c + 1, :]
        ext[c, rows : rows + SUB, :] = jnp.zeros((SUB, LANES), jnp.float32)
        ext[c, rows : rows + 1, :] = gas_rho
        ext[c, rows + 1 : rows + 3, :] = gas_vel_ref[:, cells]
        coupling = drag * gas_rho
        weight = density / gas_rho * (coupling / (1.0 + coupling))
        partial[0, c : c + 1, :] = jnp.sum(weight, axis=0, keepdims=True)
        partial[1, c : c + 1, :] = jnp.sum(weight * vel_ref[0, :, cells], axis=0, keepdims=True)
        partial[2, c : c + 1, :] = jnp.sum(weight * vel_ref[1, :, cells], axis=0, keepdims=True)
    sums[me] = partial[...].astype(jnp.bfloat16)

    def choose(fetch, target):
        for j in range(len(OFFSETS)):
            index = spread(send_ref[j : j + 1, :])
            safe = jnp.maximum(index, 0)
            lanes = safe & (LANES - 1)
            block = safe >> 7
            parts = []
            for i in range(target.shape[1] // SUB):
                value = lane_take(fetch(0, i), lanes)
                for s in range(1, groups):
                    value = jnp.where(block == s, lane_take(fetch(s, i), lanes), value)
                parts.append(jnp.where(index >= 0, value, 0.0))
            target[j] = jnp.concatenate(parts, axis=0).astype(target.dtype)

    def ghost_copy(j, source, target, send_sem, recv_sem):
        return pltpu.make_async_remote_copy(
            src_ref=source,
            dst_ref=target,
            send_sem=send_sem.at[j],
            recv_sem=recv_sem.at[j],
            device_id={"dom": lax.rem(dom + OFFSETS[j] + doms, doms)},
            device_id_type=MESH,
        )

    def rho_copy(j):
        return ghost_copy(j, ghost_rho.at[j], ext.at[groups + j], rho_send, rho_recv)

    def vel_copy(j):
        return ghost_copy(j, ghost_vel.at[j], ghost_in.at[j], vel_send, vel_recv)

    loads[9].wait()
    choose(lambda s, i: ext[s, i * SUB : (i + 1) * SUB, :], ghost_rho)

    def own_vel(s, i):
        row = i % halves * SUB
        return vel_ref[i // halves, row : row + SUB, s * LANES : (s + 1) * LANES]

    choose(own_vel, ghost_vel)
    pl.semaphore_wait(barrier, bins - 1 + len(OFFSETS))

    def peer_copy(step, source, target, send_sem, recv_sem):
        return pltpu.make_async_remote_copy(
            src_ref=source,
            dst_ref=target,
            send_sem=send_sem.at[step],
            recv_sem=recv_sem.at[step],
            device_id={"bin": lax.rem(me + step, bins)},
            device_id_type=MESH,
        )

    def peer_arrived(step, source, buffer, send_sem, recv_sem):
        sender = lax.rem(me + bins - step, bins)
        peer_copy(step, source, buffer.at[sender], send_sem, recv_sem).wait_recv()

    order = [(bins // 2 + turn) % bins for turn in (0, 1, 7, 3, 2, 5, 6, 4)]
    for j in range(len(OFFSETS)):
        rho_copy(j).start()
        vel_copy(j).start()
    for step in order[:-1]:
        peer_copy(step, sums.at[me], sums.at[me], sum_send, sum_recv).start()
    for c in range(groups):
        cells = slice(c * LANES, (c + 1) * LANES)
        coupling = drag * gas_rho_ref[c : c + 1, :]
        inverse = 1.0 / (1.0 + coupling)
        share_held[c] = coupling / (1.0 + coupling)
        for component in range(2):
            fixed[component, c] = vel_ref[component, :, cells] * inverse
            gas_held[component, c : c + 1, :] = gas_vel_ref[component : component + 1, cells]

    def pick(first_block, last_block, source, target, c, faces):
        cells = pl.ds(pl.multiple_of(c * LANES, LANES), LANES)
        for k in faces:
            safe = jnp.maximum(spread(faces_ref[k : k + 1, cells]), 0)
            lanes = safe & (LANES - 1)
            block = safe >> 7
            for r in range(0, rows, SUB):
                if first_block == 0:
                    value = lane_take(source[0, r : r + SUB, :], lanes)
                else:
                    value = target[c, k, r : r + SUB, :]
                for s in range(max(first_block, 1), last_block):
                    value = jnp.where(
                        block == s, lane_take(source[s, r : r + SUB, :], lanes), value
                    )
                target[c, k, r : r + SUB, :] = value

    def pick_all(first_block, last_block, source, target):
        def part(i, carry):
            for u in range(UNROLL):
                pick(first_block, last_block, source, target, i * UNROLL + u, range(face_count))
            return carry

        lax.fori_loop(0, groups // UNROLL, part, 0)

    total_blocks = groups + len(OFFSETS)
    loads[8].wait()
    pick_all(0, groups, ext, picked)
    for j in range(len(OFFSETS)):
        rho_copy(j).wait_recv()
        vel_copy(j).wait_recv()
    ghost_partial[...] = jnp.zeros_like(ghost_partial)
    for j in range(len(OFFSETS)):
        gas_rho = ext[groups + j, rows : rows + 1, :]
        gas_rho = jnp.where(gas_rho > 0.0, gas_rho, 1.0)
        coupling = drag * gas_rho
        inverse = 1.0 / (1.0 + coupling)
        share = coupling / (1.0 + coupling)
        share_held[groups + j] = share
        weight = ext[groups + j, 0:rows, :] / gas_rho * share
        ghost_partial[j : j + 1, :] = jnp.sum(weight, axis=0, keepdims=True)
        for component in range(2):
            vel = ghost_in[j, component * rows : (component + 1) * rows].astype(jnp.float32)
            fixed[component, groups + j] = vel * inverse
            row = (component + 1) * len(OFFSETS) + j
            ghost_partial[row : row + 1, :] = jnp.sum(weight * vel, axis=0, keepdims=True)
    ghost_sums[me] = ghost_partial[...].astype(jnp.bfloat16)
    for step in order[:-1]:
        peer_copy(step, ghost_sums.at[me], ghost_sums.at[me], add_send, add_recv).start()
    pick_all(groups, total_blocks, ext, picked)
    for i in (4, 5, 6, 10, 11):
        loads[i].wait()

    for step in range(1, bins):
        peer_arrived(step, sums.at[me], sums, sum_send, sum_recv)
    totals = sums[0].astype(jnp.float32)
    for b in range(1, bins):
        totals = totals + sums[b].astype(jnp.float32)
    gas_held[...] = (gas_held[...] + totals[1:]) / (1.0 + totals[0:1])
    for c in range(groups):
        cells = slice(c * LANES, (c + 1) * LANES)
        share = share_held[c]
        both = []
        for component in range(2):
            gas = gas_held[component, c : c + 1, :]
            gas_out[component : component + 1, cells] = gas
            dust = fixed[component, c] + share * gas
            vel_out[component, :, cells] = dust
            after[c, component * rows : (component + 1) * rows, :] = dust
            both.append(dust)
        coded[c] = join(both[0], both[1])

    pick_all(0, groups, coded, picked_vel)
    for step in range(1, bins):
        peer_arrived(step, ghost_sums.at[me], ghost_sums, add_send, add_recv)
    totals = ghost_sums[0].astype(jnp.float32)
    for b in range(1, bins):
        totals = totals + ghost_sums[b].astype(jnp.float32)
    for j in range(len(OFFSETS)):
        both = []
        for component in range(2):
            row = (component + 1) * len(OFFSETS) + j
            given = ext[groups + j, rows + 1 + component : rows + 2 + component, :]
            gas = (given + totals[row : row + 1, :]) / (1.0 + totals[j : j + 1, :])
            both.append(fixed[component, groups + j] + share_held[groups + j] * gas)
        coded[groups + j] = join(both[0], both[1])

    def advect(c):
        pick(groups, total_blocks, coded, picked_vel, c, range(face_count))
        cells = pl.ds(pl.multiple_of(c * LANES, LANES), LANES)
        valid = [spread(faces_ref[k : k + 1, cells]) >= 0 for k in range(face_count)]
        count = valid[0].astype(jnp.float32)
        for k in range(1, face_count):
            count = count + valid[k].astype(jnp.float32)
        inverse = spread(inv_ref[pl.ds(c, 1), :])
        for h in range(halves):
            first = slice(h * SUB, (h + 1) * SUB)
            second = slice(rows + h * SUB, rows + (h + 1) * SUB)
            density = ext[c, first, :]
            vel_x = after[c, first, :] - MIDDLE / STEPS
            vel_y = after[c, second, :] - MIDDLE / STEPS
            mean = jnp.where(valid[0], picked[c, 0, first, :], 0.0)
            for k in range(1, face_count):
                mean = mean + jnp.where(valid[k], picked[c, k, first, :], 0.0)
            slope = density - mean / count
            total = jnp.zeros((SUB, LANES), jnp.float32)
            for k in range(face_count):
                other = picked[c, k, first, :]
                pair = picked_vel[c, k, first, :]
                other_x = lax.shift_right_logical(pair, 16).astype(jnp.float32) * (1.0 / STEPS)
                other_y = (pair & 65535).astype(jnp.float32) * (1.0 / STEPS)
                speed = 0.5 * (
                    (vel_x + other_x) * spread(normals_ref[0, k : k + 1, cells])
                    + (vel_y + other_y) * spread(normals_ref[1, k : k + 1, cells])
                )
                limited = 0.5 * minmod(other - density, slope)
                flux = jnp.maximum(speed, 0.0) * (density + limited) + jnp.minimum(speed, 0.0) * (
                    other - limited
                )
                total = total + jnp.where(valid[k], flux, 0.0)
            moved[c, first, :] = density - inverse * total
        rounded[c] = moved[c].astype(jnp.bfloat16)

    for first in range(0, bins, UNROLL):
        for step in order[first : first + UNROLL]:
            advect(lax.rem(me + step, bins))
        for step in order[first : first + UNROLL]:
            if step > 0:
                peer = lax.rem(me + step, bins)
                peer_copy(step, rounded.at[peer], mixed.at[me], mix_send, mix_recv).start()
    mixed[me] = rounded[me]
    for step in range(1, bins):
        peer_arrived(step, rounded.at[0], mixed, mix_send, mix_recv)
    columns = mixed[...].reshape(bins * rows, LANES)
    collide = jnp.dot(kern_ref[...], columns, preferred_element_type=jnp.float32)
    rate = coag_ref[pl.ds(me, 1), :]
    loss = (rate * columns.astype(jnp.float32) * collide).astype(jnp.bfloat16)
    gain = jnp.dot(redis_ref[...], loss, preferred_element_type=jnp.float32)
    change = gain - loss.astype(jnp.float32)
    delta[...] = change.astype(jnp.bfloat16).reshape(bins, rows, LANES)
    for step in order[:-1]:
        peer = lax.rem(me + step, bins)
        peer_copy(step, delta.at[peer], back.at[me], back_send, back_recv).start()
    back[me] = delta[me]
    for step in range(1, bins):
        peer_arrived(step, delta.at[0], back, back_send, back_recv)
    for c in range(groups):
        rho_out[:, c * LANES : (c + 1) * LANES] = moved[c] + back[c].astype(jnp.float32)

    for step in range(1, bins):
        peer = lax.rem(me + step, bins)
        peer_copy(step, sums.at[me], sums.at[me], sum_send, sum_recv).wait_send()
        peer_copy(step, ghost_sums.at[me], ghost_sums.at[me], add_send, add_recv).wait_send()
        peer_copy(step, rounded.at[peer], mixed.at[me], mix_send, mix_recv).wait_send()
        peer_copy(step, delta.at[peer], back.at[me], back_send, back_recv).wait_send()
    for j in range(len(OFFSETS)):
        rho_copy(j).wait_send()
        vel_copy(j).wait_send()


def store_body(rho, vel, gas, rho_out, vel_out, gas_out, stored):
    pairs = ((rho, rho_out), (vel, vel_out), (gas, gas_out))
    copies = [
        pltpu.make_async_copy(source, target, stored.at[i])
        for i, (source, target) in enumerate(pairs)
    ]
    for copy in copies:
        copy.start()
    for copy in copies:
        copy.wait()


def body(
    dust_rho,
    dust_vel,
    gas_rho,
    gas_vel,
    normals,
    inv_volume,
    coag_rate,
    drag_coef,
    neighbours,
    send_cells,
    kernel,
    redistrib,
):
    rows, cells = dust_rho.shape
    bins = lax.axis_size("bin")
    doms = lax.axis_size("dom")
    groups = cells // LANES
    faces = neighbours.shape[0]
    ghosts = len(OFFSETS)

    def run(*refs):
        kernel_body(bins, doms, *refs)

    arrays = (
        dust_rho,
        dust_vel,
        gas_rho.reshape(groups, LANES),
        gas_vel,
        normals,
        inv_volume.reshape(groups, LANES),
        coag_rate.reshape(groups, LANES),
        drag_coef.reshape(1, rows),
        neighbours,
        send_cells.reshape(ghosts, LANES),
        kernel,
        redistrib,
    )
    shapes = (dust_rho.shape, dust_vel.shape, gas_vel.shape)
    vmem = pl.BlockSpec(memory_space=pltpu.VMEM)
    dma = pltpu.SemaphoreType.DMA
    results = pl.pallas_call(
        run,
        name="dust_step",
        out_shape=tuple(pltpu.VMEM(shape, jnp.float32) for shape in shapes),
        in_specs=[pl.BlockSpec(memory_space=pl.ANY)] * len(arrays),
        out_specs=(vmem, vmem, vmem),
        scratch_shapes=[pltpu.VMEM(array.shape, array.dtype) for array in arrays]
        + [
            dma((len(arrays),)),
            pltpu.VMEM((groups + ghosts, rows + SUB, LANES), jnp.float32),
            pltpu.VMEM((groups + ghosts, rows, LANES), jnp.int32),
            pltpu.VMEM((groups, faces, rows, LANES), jnp.float32),
            pltpu.VMEM((groups, faces, rows, LANES), jnp.int32),
            pltpu.VMEM((groups, 2 * rows, LANES), jnp.float32),
            pltpu.VMEM((3, groups, LANES), jnp.float32),
            pltpu.VMEM((bins, 3, groups, LANES), jnp.bfloat16),
            pltpu.VMEM((4 * ghosts, LANES), jnp.float32),
            pltpu.VMEM((bins, 4 * ghosts, LANES), jnp.bfloat16),
            pltpu.VMEM((2, groups, LANES), jnp.float32),
            pltpu.VMEM((2, groups + ghosts, rows, LANES), jnp.float32),
            pltpu.VMEM((groups + ghosts, rows, LANES), jnp.float32),
            pltpu.VMEM((ghosts, rows + SUB, LANES), jnp.float32),
            pltpu.VMEM((ghosts, 2 * rows, LANES), jnp.bfloat16),
            pltpu.VMEM((ghosts, 2 * rows, LANES), jnp.bfloat16),
            pltpu.VMEM((groups, rows, LANES), jnp.float32),
            pltpu.VMEM((groups, rows, LANES), jnp.bfloat16),
            pltpu.VMEM((bins, rows, LANES), jnp.bfloat16),
            pltpu.VMEM((bins, rows, LANES), jnp.bfloat16),
            pltpu.VMEM((bins, rows, LANES), jnp.bfloat16),
            dma((bins,)),
            dma((bins,)),
            dma((bins,)),
            dma((bins,)),
            dma((ghosts,)),
            dma((ghosts,)),
            dma((ghosts,)),
            dma((ghosts,)),
            dma((bins,)),
            dma((bins,)),
            dma((bins,)),
            dma((bins,)),
        ],
        compiler_params=pltpu.CompilerParams(collective_id=0, has_side_effects=True),
    )(*arrays)
    return pl.pallas_call(
        store_body,
        name="dust_store",
        out_shape=tuple(jax.ShapeDtypeStruct(shape, jnp.float32) for shape in shapes),
        in_specs=[vmem] * 3,
        out_specs=(pl.BlockSpec(memory_space=pl.ANY),) * 3,
        scratch_shapes=[dma((3,))],
        compiler_params=pltpu.CompilerParams(vmem_limit_bytes=1 << 20),
    )(*results)


def solution(mesh):
    placed = (
        P("bin", "dom"),
        P(None, "bin", "dom"),
        P("dom"),
        P(None, "dom"),
        P(None, None, "dom"),
        P("dom"),
        P("dom"),
        P("bin"),
        P(None, "dom"),
        P("dom", None, None),
        P(),
        P(),
    )
    return jax.shard_map(
        body,
        mesh=mesh,
        in_specs=placed,
        out_specs=(P("bin", "dom"), P(None, "bin", "dom"), P(None, "dom")),
        check_vma=False,
    )
```

```python
import jax
import jax.numpy as jnp
from jax import lax
from jax.experimental import pallas as pl
from jax.experimental.pallas import tpu as pltpu
from jax.sharding import PartitionSpec as P

OFFSETS = (1, -1, 2, -2)
LANES = 128
SUB = 8
MESH = pl.DeviceIdType.MESH
STEPS = 8191.0
MIDDLE = 32768.0
UNROLL = 4


def spread(row):
    return jnp.broadcast_to(row, (SUB, LANES))


def lane_take(block, lanes):
    return jnp.take_along_axis(block, lanes, axis=1, mode="promise_in_bounds")


def join(vel_x, vel_y):
    first = (vel_x * STEPS + (MIDDLE + 0.5)).astype(jnp.int32)
    second = (vel_y * STEPS + (MIDDLE + 0.5)).astype(jnp.int32)
    return first * 65536 + second


def minmod(first, second):
    return jnp.maximum(jnp.minimum(first, second), 0.0) + jnp.minimum(
        jnp.maximum(first, second), 0.0
    )


def kernel_body(
    bins,
    doms,
    *refs,
):
    held = refs[:12]
    rho_out, vel_out, gas_out = refs[12:15]
    inputs = refs[15:27]
    loaded = refs[27]
    (
        rho_ref,
        vel_ref,
        gas_rho_ref,
        gas_vel_ref,
        normals_ref,
        inv_ref,
        coag_ref,
        drag_ref,
        faces_ref,
        send_ref,
        kern_ref,
        redis_ref,
    ) = inputs
    (
        ext,
        coded,
        picked,
        picked_vel,
        outward,
        inward,
        base,
        partial,
        sums,
        gas_held,
        fixed,
        share_held,
        ghost_rho,
        ghost_vel,
        ghost_in,
        moved,
        rounded,
        mixed,
        delta,
        back,
        sum_send,
        sum_recv,
        rho_send,
        rho_recv,
        vel_send,
        vel_recv,
        mix_send,
        mix_recv,
        back_send,
        back_recv,
    ) = refs[28:]
    rows = rho_ref.shape[0]
    groups = rho_ref.shape[1] // LANES
    face_count = faces_ref.shape[0]
    halves = rows // SUB
    me = lax.axis_index("bin")
    dom = lax.axis_index("dom")

    barrier = pltpu.get_barrier_semaphore()
    for step in range(1, bins):
        pl.semaphore_signal(
            barrier, inc=1, device_id={"bin": lax.rem(me + step, bins)}, device_id_type=MESH
        )
    for offset in OFFSETS:
        pl.semaphore_signal(
            barrier,
            inc=1,
            device_id={"dom": lax.rem(dom + offset + doms, doms)},
            device_id_type=MESH,
        )

    loads = [
        pltpu.make_async_copy(held[i], inputs[i], loaded.at[i]) for i in range(len(inputs))
    ]
    for i in (0, 2, 7, 9, 1, 8, 3, 4, 5, 6, 10, 11):
        loads[i].start()
    for i in (0, 2, 7, 1):
        loads[i].wait()

    diagonal = lax.broadcasted_iota(jnp.int32, (rows, rows), 0) == lax.broadcasted_iota(
        jnp.int32, (rows, rows), 1
    )
    drag = jnp.sum(
        jnp.where(diagonal, jnp.broadcast_to(drag_ref[...], (rows, rows)), 0.0),
        axis=1,
        keepdims=True,
    )

    for c in range(groups):
        cells = slice(c * LANES, (c + 1) * LANES)
        density = rho_ref[:, cells]
        ext[c, 0:rows, :] = density
        gas_rho = gas_rho_ref[c : c + 1, :]
        coupling = drag * gas_rho
        weight = density / gas_rho * (coupling / (1.0 + coupling))
        partial[0, c : c + 1, :] = jnp.sum(weight, axis=0, keepdims=True)
        partial[1, c : c + 1, :] = jnp.sum(weight * vel_ref[0, :, cells], axis=0, keepdims=True)
        partial[2, c : c + 1, :] = jnp.sum(weight * vel_ref[1, :, cells], axis=0, keepdims=True)
    sums[me] = partial[...].astype(jnp.bfloat16)

    def choose(first_row, target):
        for j in range(len(OFFSETS)):
            index = spread(send_ref[j : j + 1, :])
            safe = jnp.maximum(index, 0)
            lanes = safe & (LANES - 1)
            block = safe >> 7
            parts = []
            for r in range(first_row, first_row + target.shape[1], SUB):
                value = lane_take(ext[0, r : r + SUB, :], lanes)
                for s in range(1, groups):
                    value = jnp.where(
                        block == s, lane_take(ext[s, r : r + SUB, :], lanes), value
                    )
                parts.append(jnp.where(index >= 0, value, 0.0))
            target[j] = jnp.concatenate(parts, axis=0).astype(target.dtype)

    def ghost_copy(j, source, target, send_sem, recv_sem):
        return pltpu.make_async_remote_copy(
            src_ref=source,
            dst_ref=target,
            send_sem=send_sem.at[j],
            recv_sem=recv_sem.at[j],
            device_id={"dom": lax.rem(dom + OFFSETS[j] + doms, doms)},
            device_id_type=MESH,
        )

    def rho_copy(j):
        target = ext.at[groups + j, 0:rows]
        return ghost_copy(j, ghost_rho.at[j], target, rho_send, rho_recv)

    def vel_copy(j):
        return ghost_copy(j, ghost_vel.at[j], ghost_in.at[j], vel_send, vel_recv)

    loads[9].wait()
    choose(0, ghost_rho)
    pl.semaphore_wait(barrier, bins - 1 + len(OFFSETS))

    def peer_copy(step, source, target, send_sem, recv_sem):
        return pltpu.make_async_remote_copy(
            src_ref=source,
            dst_ref=target,
            send_sem=send_sem.at[step],
            recv_sem=recv_sem.at[step],
            device_id={"bin": lax.rem(me + step, bins)},
            device_id_type=MESH,
        )

    def peer_arrived(step, source, buffer, send_sem, recv_sem):
        sender = lax.rem(me + bins - step, bins)
        peer_copy(step, source, buffer.at[sender], send_sem, recv_sem).wait_recv()

    order = [(bins // 2 + turn) % bins for turn in (0, 1, 7, 3, 2, 5, 6, 4)]
    for step in order[:-1]:
        peer_copy(step, sums.at[me], sums.at[me], sum_send, sum_recv).start()
    for j in range(len(OFFSETS)):
        rho_copy(j).start()
    loads[3].wait()
    for c in range(groups):
        cells = slice(c * LANES, (c + 1) * LANES)
        coupling = drag * gas_rho_ref[c : c + 1, :]
        inverse = 1.0 / (1.0 + coupling)
        share_held[c] = coupling / (1.0 + coupling)
        for component in range(2):
            fixed[component, c] = vel_ref[component, :, cells] * inverse
            gas_held[component, c : c + 1, :] = gas_vel_ref[component : component + 1, cells]

    def pick(first_block, last_block, source, target, c, faces):
        cells = pl.ds(pl.multiple_of(c * LANES, LANES), LANES)
        for k in faces:
            safe = jnp.maximum(spread(faces_ref[k : k + 1, cells]), 0)
            lanes = safe & (LANES - 1)
            block = safe >> 7
            for r in range(0, rows, SUB):
                if first_block == 0:
                    value = lane_take(source[0, r : r + SUB, :], lanes)
                else:
                    value = target[c, k, r : r + SUB, :]
                for s in range(max(first_block, 1), last_block):
                    value = jnp.where(
                        block == s, lane_take(source[s, r : r + SUB, :], lanes), value
                    )
                target[c, k, r : r + SUB, :] = value

    def pick_all(first_block, last_block, source, target):
        def part(i, carry):
            for u in range(UNROLL):
                pick(first_block, last_block, source, target, i * UNROLL + u, range(face_count))
            return carry

        lax.fori_loop(0, groups // UNROLL, part, 0)

    total_blocks = groups + len(OFFSETS)
    loads[8].wait()
    pick_all(0, groups, ext, picked)
    for j in range(len(OFFSETS)):
        rho_copy(j).wait_recv()
    pick_all(groups, total_blocks, ext, picked)
    for i in (4, 5, 6, 10, 11):
        loads[i].wait()

    def limit(c, carry):
        cells = pl.ds(pl.multiple_of(c * LANES, LANES), LANES)
        valid = [spread(faces_ref[k : k + 1, cells]) >= 0 for k in range(face_count)]
        count = valid[0].astype(jnp.float32)
        for k in range(1, face_count):
            count = count + valid[k].astype(jnp.float32)
        for h in range(halves):
            first = slice(h * SUB, (h + 1) * SUB)
            density = ext[c, first, :]
            mean = jnp.where(valid[0], picked[c, 0, first, :], 0.0)
            for k in range(1, face_count):
                mean = mean + jnp.where(valid[k], picked[c, k, first, :], 0.0)
            slope = density - mean / count
            for k in range(face_count):
                other = picked[c, k, first, :]
                limited = 0.5 * minmod(other - density, slope)
                outward[c, k, first, :] = jnp.where(valid[k], density + limited, 0.0)
                inward[c, k, first, :] = jnp.where(valid[k], other - limited, 0.0)
        return carry

    lax.fori_loop(0, groups, limit, 0)

    for step in range(1, bins):
        peer_arrived(step, sums.at[me], sums, sum_send, sum_recv)
    totals = sums[0].astype(jnp.float32)
    for b in range(1, bins):
        totals = totals + sums[b].astype(jnp.float32)
    gas_held[...] = (gas_held[...] + totals[1:]) / (1.0 + totals[0:1])
    for c in range(groups):
        cells = slice(c * LANES, (c + 1) * LANES)
        share = share_held[c]
        both = []
        for component in range(2):
            gas = gas_held[component, c : c + 1, :]
            gas_out[component : component + 1, cells] = gas
            dust = fixed[component, c] + share * gas
            vel_out[component, :, cells] = dust
            ext[c, (component + 1) * rows : (component + 2) * rows, :] = dust
            both.append(dust)
        coded[c] = join(both[0], both[1])

    choose(rows, ghost_vel)
    for j in range(len(OFFSETS)):
        vel_copy(j).start()
    pick_all(0, groups, coded, picked_vel)

    def prepare(c, carry):
        cells = pl.ds(pl.multiple_of(c * LANES, LANES), LANES)
        for h in range(halves):
            first = slice(h * SUB, (h + 1) * SUB)
            vel_x = ext[c, rows + h * SUB : rows + (h + 1) * SUB, :] - MIDDLE / STEPS
            vel_y = ext[c, 2 * rows + h * SUB : 2 * rows + (h + 1) * SUB, :] - MIDDLE / STEPS
            for k in range(face_count):
                base[c, k, first, :] = 0.5 * (
                    vel_x * spread(normals_ref[0, k : k + 1, cells])
                    + vel_y * spread(normals_ref[1, k : k + 1, cells])
                )
        return carry

    lax.fori_loop(0, groups, prepare, 0)
    for j in range(len(OFFSETS)):
        vel_copy(j).wait_recv()
        coded[groups + j] = join(
            ghost_in[j, 0:rows].astype(jnp.float32),
            ghost_in[j, rows : 2 * rows].astype(jnp.float32),
        )

    def advect(c):
        pick(groups, total_blocks, coded, picked_vel, c, range(face_count))
        cells = pl.ds(pl.multiple_of(c * LANES, LANES), LANES)
        volume = spread(inv_ref[pl.ds(c, 1), :])
        total = [jnp.zeros((SUB, LANES), jnp.float32) for h in range(halves)]
        for k in range(face_count):
            normal_x = spread(normals_ref[0, k : k + 1, cells]) * (0.5 / STEPS)
            normal_y = spread(normals_ref[1, k : k + 1, cells]) * (0.5 / STEPS)
            for h in range(halves):
                first = slice(h * SUB, (h + 1) * SUB)
                pair = picked_vel[c, k, first, :]
                other_x = lax.shift_right_logical(pair, 16).astype(jnp.float32)
                other_y = (pair & 65535).astype(jnp.float32)
                speed = base[c, k, first, :] + (other_x * normal_x + other_y * normal_y)
                total[h] = total[h] + (
                    jnp.maximum(speed, 0.0) * outward[c, k, first, :]
                    + jnp.minimum(speed, 0.0) * inward[c, k, first, :]
                )
        for h in range(halves):
            first = slice(h * SUB, (h + 1) * SUB)
            moved[c, first, :] = ext[c, first, :] - volume * total[h]
        rounded[c] = moved[c].astype(jnp.bfloat16)

    for first in range(0, bins, UNROLL):
        for step in order[first : first + UNROLL]:
            advect(lax.rem(me + step, bins))
        for step in order[first : first + UNROLL]:
            if step > 0:
                peer = lax.rem(me + step, bins)
                peer_copy(step, rounded.at[peer], mixed.at[me], mix_send, mix_recv).start()
    mixed[me] = rounded[me]
    for step in range(1, bins):
        peer_arrived(step, rounded.at[0], mixed, mix_send, mix_recv)
    columns = mixed[...].reshape(bins * rows, LANES)
    collide = jnp.dot(kern_ref[...], columns, preferred_element_type=jnp.float32)
    rate = coag_ref[pl.ds(me, 1), :]
    loss = (rate * columns.astype(jnp.float32) * collide).astype(jnp.bfloat16)
    gain = jnp.dot(redis_ref[...], loss, preferred_element_type=jnp.float32)
    change = gain - loss.astype(jnp.float32)
    delta[...] = change.astype(jnp.bfloat16).reshape(bins, rows, LANES)
    for step in order[:-1]:
        peer = lax.rem(me + step, bins)
        peer_copy(step, delta.at[peer], back.at[me], back_send, back_recv).start()
    back[me] = delta[me]
    for step in range(1, bins):
        peer_arrived(step, delta.at[0], back, back_send, back_recv)
    for c in range(groups):
        rho_out[:, c * LANES : (c + 1) * LANES] = moved[c] + back[c].astype(jnp.float32)

    for step in range(1, bins):
        peer = lax.rem(me + step, bins)
        peer_copy(step, sums.at[me], sums.at[me], sum_send, sum_recv).wait_send()
        peer_copy(step, rounded.at[peer], mixed.at[me], mix_send, mix_recv).wait_send()
        peer_copy(step, delta.at[peer], back.at[me], back_send, back_recv).wait_send()
    for j in range(len(OFFSETS)):
        rho_copy(j).wait_send()
        vel_copy(j).wait_send()


def store_body(rho, vel, gas, rho_out, vel_out, gas_out, stored):
    pairs = ((rho, rho_out), (vel, vel_out), (gas, gas_out))
    copies = [
        pltpu.make_async_copy(source, target, stored.at[i])
        for i, (source, target) in enumerate(pairs)
    ]
    for copy in copies:
        copy.start()
    for copy in copies:
        copy.wait()


def body(
    dust_rho,
    dust_vel,
    gas_rho,
    gas_vel,
    normals,
    inv_volume,
    coag_rate,
    drag_coef,
    neighbours,
    send_cells,
    kernel,
    redistrib,
):
    rows, cells = dust_rho.shape
    bins = lax.axis_size("bin")
    doms = lax.axis_size("dom")
    groups = cells // LANES
    faces = neighbours.shape[0]
    ghosts = len(OFFSETS)

    def run(*refs):
        kernel_body(bins, doms, *refs)

    arrays = (
        dust_rho,
        dust_vel,
        gas_rho.reshape(groups, LANES),
        gas_vel,
        normals,
        inv_volume.reshape(groups, LANES),
        coag_rate.reshape(groups, LANES),
        drag_coef.reshape(1, rows),
        neighbours,
        send_cells.reshape(ghosts, LANES),
        kernel,
        redistrib,
    )
    shapes = (dust_rho.shape, dust_vel.shape, gas_vel.shape)
    vmem = pl.BlockSpec(memory_space=pltpu.VMEM)
    dma = pltpu.SemaphoreType.DMA
    results = pl.pallas_call(
        run,
        name="dust_step",
        out_shape=tuple(pltpu.VMEM(shape, jnp.float32) for shape in shapes),
        in_specs=[pl.BlockSpec(memory_space=pl.ANY)] * len(arrays),
        out_specs=(vmem, vmem, vmem),
        scratch_shapes=[pltpu.VMEM(array.shape, array.dtype) for array in arrays]
        + [
            dma((len(arrays),)),
            pltpu.VMEM((groups + ghosts, 3 * rows, LANES), jnp.float32),
            pltpu.VMEM((groups + ghosts, rows, LANES), jnp.int32),
            pltpu.VMEM((groups, faces, rows, LANES), jnp.float32),
            pltpu.VMEM((groups, faces, rows, LANES), jnp.int32),
            pltpu.VMEM((groups, faces, rows, LANES), jnp.float32),
            pltpu.VMEM((groups, faces, rows, LANES), jnp.float32),
            pltpu.VMEM((groups, faces, rows, LANES), jnp.float32),
            pltpu.VMEM((3, groups, LANES), jnp.float32),
            pltpu.VMEM((bins, 3, groups, LANES), jnp.bfloat16),
            pltpu.VMEM((2, groups, LANES), jnp.float32),
            pltpu.VMEM((2, groups, rows, LANES), jnp.float32),
            pltpu.VMEM((groups, rows, LANES), jnp.float32),
            pltpu.VMEM((ghosts, rows, LANES), jnp.float32),
            pltpu.VMEM((ghosts, 2 * rows, LANES), jnp.bfloat16),
            pltpu.VMEM((ghosts, 2 * rows, LANES), jnp.bfloat16),
            pltpu.VMEM((groups, rows, LANES), jnp.float32),
            pltpu.VMEM((groups, rows, LANES), jnp.bfloat16),
            pltpu.VMEM((bins, rows, LANES), jnp.bfloat16),
            pltpu.VMEM((bins, rows, LANES), jnp.bfloat16),
            pltpu.VMEM((bins, rows, LANES), jnp.bfloat16),
            dma((bins,)),
            dma((bins,)),
            dma((ghosts,)),
            dma((ghosts,)),
            dma((ghosts,)),
            dma((ghosts,)),
            dma((bins,)),
            dma((bins,)),
            dma((bins,)),
            dma((bins,)),
        ],
        compiler_params=pltpu.CompilerParams(collective_id=0, has_side_effects=True),
    )(*arrays)
    return pl.pallas_call(
        store_body,
        name="dust_store",
        out_shape=tuple(jax.ShapeDtypeStruct(shape, jnp.float32) for shape in shapes),
        in_specs=[vmem] * 3,
        out_specs=(pl.BlockSpec(memory_space=pl.ANY),) * 3,
        scratch_shapes=[dma((3,))],
        compiler_params=pltpu.CompilerParams(vmem_limit_bytes=1 << 20),
    )(*results)


def solution(mesh):
    placed = (
        P("bin", "dom"),
        P(None, "bin", "dom"),
        P("dom"),
        P(None, "dom"),
        P(None, None, "dom"),
        P("dom"),
        P("dom"),
        P("bin"),
        P(None, "dom"),
        P("dom", None, None),
        P(),
        P(),
    )
    return jax.shard_map(
        body,
        mesh=mesh,
        in_specs=placed,
        out_specs=(P("bin", "dom"), P(None, "bin", "dom"), P(None, "dom")),
        check_vma=False,
    )
```

```python
import jax
import jax.numpy as jnp
from jax import lax
from jax.experimental import pallas as pl
from jax.experimental.pallas import tpu as pltpu
from jax.sharding import PartitionSpec as P

OFFSETS = (1, -1, 2, -2)
LANES = 128
SUB = 8
MESH = pl.DeviceIdType.MESH
STEPS = 8191.0
MIDDLE = 32768.0
UNROLL = 4


def spread(row):
    return jnp.broadcast_to(row, (SUB, LANES))


def lane_take(block, lanes):
    return jnp.take_along_axis(block, lanes, axis=1, mode="promise_in_bounds")


def join(vel_x, vel_y):
    first = (vel_x * STEPS + (MIDDLE + 0.5)).astype(jnp.int32)
    second = (vel_y * STEPS + (MIDDLE + 0.5)).astype(jnp.int32)
    return first * 65536 + second


def minmod(first, second):
    return jnp.maximum(jnp.minimum(first, second), 0.0) + jnp.minimum(
        jnp.maximum(first, second), 0.0
    )


def kernel_body(
    bins,
    doms,
    *refs,
):
    held = refs[:12]
    rho_out, vel_out, gas_out = refs[12:15]
    inputs = refs[15:27]
    loaded = refs[27]
    (
        rho_ref,
        vel_ref,
        gas_rho_ref,
        gas_vel_ref,
        normals_ref,
        inv_ref,
        coag_ref,
        drag_ref,
        faces_ref,
        send_ref,
        kern_ref,
        redis_ref,
    ) = inputs
    (
        ext,
        coded,
        picked,
        picked_vel,
        partial,
        sums,
        gas_held,
        fixed,
        share_held,
        ghost_rho,
        ghost_vel,
        ghost_in,
        moved,
        rounded,
        mixed,
        delta,
        back,
        sum_send,
        sum_recv,
        rho_send,
        rho_recv,
        vel_send,
        vel_recv,
        mix_send,
        mix_recv,
        back_send,
        back_recv,
    ) = refs[28:]
    rows = rho_ref.shape[0]
    groups = rho_ref.shape[1] // LANES
    face_count = faces_ref.shape[0]
    halves = rows // SUB
    me = lax.axis_index("bin")
    dom = lax.axis_index("dom")

    barrier = pltpu.get_barrier_semaphore()
    for step in range(1, bins):
        pl.semaphore_signal(
            barrier, inc=1, device_id={"bin": lax.rem(me + step, bins)}, device_id_type=MESH
        )
    for offset in OFFSETS:
        pl.semaphore_signal(
            barrier,
            inc=1,
            device_id={"dom": lax.rem(dom + offset + doms, doms)},
            device_id_type=MESH,
        )

    loads = [
        pltpu.make_async_copy(held[i], inputs[i], loaded.at[i]) for i in range(len(inputs))
    ]
    for i in (0, 2, 7, 9, 1, 8, 3, 4, 5, 6, 10, 11):
        loads[i].start()
    for i in (0, 2, 7, 1):
        loads[i].wait()

    diagonal = lax.broadcasted_iota(jnp.int32, (rows, rows), 0) == lax.broadcasted_iota(
        jnp.int32, (rows, rows), 1
    )
    drag = jnp.sum(
        jnp.where(diagonal, jnp.broadcast_to(drag_ref[...], (rows, rows)), 0.0),
        axis=1,
        keepdims=True,
    )

    for c in range(groups):
        cells = slice(c * LANES, (c + 1) * LANES)
        density = rho_ref[:, cells]
        ext[c, 0:rows, :] = density
        gas_rho = gas_rho_ref[c : c + 1, :]
        coupling = drag * gas_rho
        weight = density / gas_rho * (coupling / (1.0 + coupling))
        partial[0, c : c + 1, :] = jnp.sum(weight, axis=0, keepdims=True)
        partial[1, c : c + 1, :] = jnp.sum(weight * vel_ref[0, :, cells], axis=0, keepdims=True)
        partial[2, c : c + 1, :] = jnp.sum(weight * vel_ref[1, :, cells], axis=0, keepdims=True)
    sums[me] = partial[...].astype(jnp.bfloat16)

    def choose(first_row, target):
        for j in range(len(OFFSETS)):
            index = spread(send_ref[j : j + 1, :])
            safe = jnp.maximum(index, 0)
            lanes = safe & (LANES - 1)
            block = safe >> 7
            parts = []
            for r in range(first_row, first_row + target.shape[1], SUB):
                value = lane_take(ext[0, r : r + SUB, :], lanes)
                for s in range(1, groups):
                    value = jnp.where(
                        block == s, lane_take(ext[s, r : r + SUB, :], lanes), value
                    )
                parts.append(jnp.where(index >= 0, value, 0.0))
            target[j] = jnp.concatenate(parts, axis=0).astype(target.dtype)

    def ghost_copy(j, source, target, send_sem, recv_sem):
        return pltpu.make_async_remote_copy(
            src_ref=source,
            dst_ref=target,
            send_sem=send_sem.at[j],
            recv_sem=recv_sem.at[j],
            device_id={"dom": lax.rem(dom + OFFSETS[j] + doms, doms)},
            device_id_type=MESH,
        )

    def rho_copy(j):
        target = ext.at[groups + j, 0:rows]
        return ghost_copy(j, ghost_rho.at[j], target, rho_send, rho_recv)

    def vel_copy(j):
        return ghost_copy(j, ghost_vel.at[j], ghost_in.at[j], vel_send, vel_recv)

    loads[9].wait()
    choose(0, ghost_rho)
    pl.semaphore_wait(barrier, bins - 1 + len(OFFSETS))

    def peer_copy(step, source, target, send_sem, recv_sem):
        return pltpu.make_async_remote_copy(
            src_ref=source,
            dst_ref=target,
            send_sem=send_sem.at[step],
            recv_sem=recv_sem.at[step],
            device_id={"bin": lax.rem(me + step, bins)},
            device_id_type=MESH,
        )

    def peer_arrived(step, source, buffer, send_sem, recv_sem):
        sender = lax.rem(me + bins - step, bins)
        peer_copy(step, source, buffer.at[sender], send_sem, recv_sem).wait_recv()

    order = [(bins // 2 + turn) % bins for turn in (0, 1, 7, 3, 2, 5, 6, 4)]
    odd = lax.rem(dom, 2)

    def turned(step):
        return step + odd * (bins - 2 * step)

    for step in order[:-1]:
        peer_copy(turned(step), sums.at[me], sums.at[me], sum_send, sum_recv).start()
    for j in range(len(OFFSETS)):
        rho_copy(j).start()
    loads[3].wait()
    for c in range(groups):
        cells = slice(c * LANES, (c + 1) * LANES)
        coupling = drag * gas_rho_ref[c : c + 1, :]
        inverse = 1.0 / (1.0 + coupling)
        share_held[c] = coupling / (1.0 + coupling)
        for component in range(2):
            fixed[component, c] = vel_ref[component, :, cells] * inverse
            gas_held[component, c : c + 1, :] = gas_vel_ref[component : component + 1, cells]

    def pick(first_block, last_block, source, target, c, faces):
        cells = pl.ds(pl.multiple_of(c * LANES, LANES), LANES)
        for k in faces:
            safe = jnp.maximum(spread(faces_ref[k : k + 1, cells]), 0)
            lanes = safe & (LANES - 1)
            block = safe >> 7
            for r in range(0, rows, SUB):
                if first_block == 0:
                    value = lane_take(source[0, r : r + SUB, :], lanes)
                else:
                    value = target[c, k, r : r + SUB, :]
                for s in range(max(first_block, 1), last_block):
                    value = jnp.where(
                        block == s, lane_take(source[s, r : r + SUB, :], lanes), value
                    )
                target[c, k, r : r + SUB, :] = value

    def pick_all(first_block, last_block, source, target):
        def part(i, carry):
            for u in range(UNROLL):
                pick(first_block, last_block, source, target, i * UNROLL + u, range(face_count))
            return carry

        lax.fori_loop(0, groups // UNROLL, part, 0)

    total_blocks = groups + len(OFFSETS)
    loads[8].wait()
    pick_all(0, groups, ext, picked)
    for j in range(len(OFFSETS)):
        rho_copy(j).wait_recv()
    pick_all(groups, total_blocks, ext, picked)
    for i in (4, 5, 6, 10, 11):
        loads[i].wait()

    for step in range(1, bins):
        peer_arrived(step, sums.at[me], sums, sum_send, sum_recv)
    totals = sums[0].astype(jnp.float32)
    for b in range(1, bins):
        totals = totals + sums[b].astype(jnp.float32)
    gas_held[...] = (gas_held[...] + totals[1:]) / (1.0 + totals[0:1])
    for c in range(groups):
        cells = slice(c * LANES, (c + 1) * LANES)
        share = share_held[c]
        both = []
        for component in range(2):
            gas = gas_held[component, c : c + 1, :]
            gas_out[component : component + 1, cells] = gas
            dust = fixed[component, c] + share * gas
            vel_out[component, :, cells] = dust
            ext[c, (component + 1) * rows : (component + 2) * rows, :] = dust
            both.append(dust)
        coded[c] = join(both[0], both[1])

    choose(rows, ghost_vel)
    for j in range(len(OFFSETS)):
        vel_copy(j).start()
    pick_all(0, groups, coded, picked_vel)
    for j in range(len(OFFSETS)):
        vel_copy(j).wait_recv()
        coded[groups + j] = join(
            ghost_in[j, 0:rows].astype(jnp.float32),
            ghost_in[j, rows : 2 * rows].astype(jnp.float32),
        )

    def advect(c):
        pick(groups, total_blocks, coded, picked_vel, c, range(face_count))
        cells = pl.ds(pl.multiple_of(c * LANES, LANES), LANES)
        valid = [spread(faces_ref[k : k + 1, cells]) >= 0 for k in range(face_count)]
        count = valid[0].astype(jnp.float32)
        for k in range(1, face_count):
            count = count + valid[k].astype(jnp.float32)
        inverse = spread(inv_ref[pl.ds(c, 1), :])
        for h in range(halves):
            first = slice(h * SUB, (h + 1) * SUB)
            second = slice(rows + h * SUB, rows + (h + 1) * SUB)
            third = slice(2 * rows + h * SUB, 2 * rows + (h + 1) * SUB)
            density = ext[c, first, :]
            vel_x = ext[c, second, :] - MIDDLE / STEPS
            vel_y = ext[c, third, :] - MIDDLE / STEPS
            mean = jnp.where(valid[0], picked[c, 0, first, :], 0.0)
            for k in range(1, face_count):
                mean = mean + jnp.where(valid[k], picked[c, k, first, :], 0.0)
            slope = density - mean / count
            total = jnp.zeros((SUB, LANES), jnp.float32)
            for k in range(face_count):
                other = picked[c, k, first, :]
                pair = picked_vel[c, k, first, :]
                other_x = lax.shift_right_logical(pair, 16).astype(jnp.float32) * (1.0 / STEPS)
                other_y = (pair & 65535).astype(jnp.float32) * (1.0 / STEPS)
                speed = 0.5 * (
                    (vel_x + other_x) * spread(normals_ref[0, k : k + 1, cells])
                    + (vel_y + other_y) * spread(normals_ref[1, k : k + 1, cells])
                )
                limited = 0.5 * minmod(other - density, slope)
                flux = jnp.maximum(speed, 0.0) * (density + limited) + jnp.minimum(speed, 0.0) * (
                    other - limited
                )
                total = total + jnp.where(valid[k], flux, 0.0)
            moved[c, first, :] = density - inverse * total
        rounded[c] = moved[c].astype(jnp.bfloat16)

    for first in range(0, bins, UNROLL):
        for step in order[first : first + UNROLL]:
            advect(lax.rem(me + turned(step), bins))
        for step in order[first : first + UNROLL]:
            if step > 0:
                peer = lax.rem(me + turned(step), bins)
                peer_copy(turned(step), rounded.at[peer], mixed.at[me], mix_send, mix_recv).start()
    mixed[me] = rounded[me]
    for step in range(1, bins):
        peer_arrived(step, rounded.at[0], mixed, mix_send, mix_recv)
    columns = mixed[...].reshape(bins * rows, LANES)
    collide = jnp.dot(kern_ref[...], columns, preferred_element_type=jnp.float32)
    rate = coag_ref[pl.ds(me, 1), :]
    loss = (rate * columns.astype(jnp.float32) * collide).astype(jnp.bfloat16)
    gain = jnp.dot(redis_ref[...], loss, preferred_element_type=jnp.float32)
    change = gain - loss.astype(jnp.float32)
    delta[...] = change.astype(jnp.bfloat16).reshape(bins, rows, LANES)
    for step in order[:-1]:
        peer = lax.rem(me + turned(step), bins)
        peer_copy(turned(step), delta.at[peer], back.at[me], back_send, back_recv).start()
    back[me] = delta[me]
    for step in range(1, bins):
        peer_arrived(step, delta.at[0], back, back_send, back_recv)
    for c in range(groups):
        rho_out[:, c * LANES : (c + 1) * LANES] = moved[c] + back[c].astype(jnp.float32)

    for step in range(1, bins):
        peer = lax.rem(me + step, bins)
        peer_copy(step, sums.at[me], sums.at[me], sum_send, sum_recv).wait_send()
        peer_copy(step, rounded.at[peer], mixed.at[me], mix_send, mix_recv).wait_send()
        peer_copy(step, delta.at[peer], back.at[me], back_send, back_recv).wait_send()
    for j in range(len(OFFSETS)):
        rho_copy(j).wait_send()
        vel_copy(j).wait_send()


def store_body(rho, vel, gas, rho_out, vel_out, gas_out, stored):
    pairs = ((rho, rho_out), (vel, vel_out), (gas, gas_out))
    copies = [
        pltpu.make_async_copy(source, target, stored.at[i])
        for i, (source, target) in enumerate(pairs)
    ]
    for copy in copies:
        copy.start()
    for copy in copies:
        copy.wait()


def body(
    dust_rho,
    dust_vel,
    gas_rho,
    gas_vel,
    normals,
    inv_volume,
    coag_rate,
    drag_coef,
    neighbours,
    send_cells,
    kernel,
    redistrib,
):
    rows, cells = dust_rho.shape
    bins = lax.axis_size("bin")
    doms = lax.axis_size("dom")
    groups = cells // LANES
    faces = neighbours.shape[0]
    ghosts = len(OFFSETS)

    def run(*refs):
        kernel_body(bins, doms, *refs)

    arrays = (
        dust_rho,
        dust_vel,
        gas_rho.reshape(groups, LANES),
        gas_vel,
        normals,
        inv_volume.reshape(groups, LANES),
        coag_rate.reshape(groups, LANES),
        drag_coef.reshape(1, rows),
        neighbours,
        send_cells.reshape(ghosts, LANES),
        kernel,
        redistrib,
    )
    shapes = (dust_rho.shape, dust_vel.shape, gas_vel.shape)
    vmem = pl.BlockSpec(memory_space=pltpu.VMEM)
    dma = pltpu.SemaphoreType.DMA
    results = pl.pallas_call(
        run,
        name="dust_step",
        out_shape=tuple(pltpu.VMEM(shape, jnp.float32) for shape in shapes),
        in_specs=[pl.BlockSpec(memory_space=pl.ANY)] * len(arrays),
        out_specs=(vmem, vmem, vmem),
        scratch_shapes=[pltpu.VMEM(array.shape, array.dtype) for array in arrays]
        + [
            dma((len(arrays),)),
            pltpu.VMEM((groups + ghosts, 3 * rows, LANES), jnp.float32),
            pltpu.VMEM((groups + ghosts, rows, LANES), jnp.int32),
            pltpu.VMEM((groups, faces, rows, LANES), jnp.float32),
            pltpu.VMEM((groups, faces, rows, LANES), jnp.int32),
            pltpu.VMEM((3, groups, LANES), jnp.float32),
            pltpu.VMEM((bins, 3, groups, LANES), jnp.bfloat16),
            pltpu.VMEM((2, groups, LANES), jnp.float32),
            pltpu.VMEM((2, groups, rows, LANES), jnp.float32),
            pltpu.VMEM((groups, rows, LANES), jnp.float32),
            pltpu.VMEM((ghosts, rows, LANES), jnp.float32),
            pltpu.VMEM((ghosts, 2 * rows, LANES), jnp.bfloat16),
            pltpu.VMEM((ghosts, 2 * rows, LANES), jnp.bfloat16),
            pltpu.VMEM((groups, rows, LANES), jnp.float32),
            pltpu.VMEM((groups, rows, LANES), jnp.bfloat16),
            pltpu.VMEM((bins, rows, LANES), jnp.bfloat16),
            pltpu.VMEM((bins, rows, LANES), jnp.bfloat16),
            pltpu.VMEM((bins, rows, LANES), jnp.bfloat16),
            dma((bins,)),
            dma((bins,)),
            dma((ghosts,)),
            dma((ghosts,)),
            dma((ghosts,)),
            dma((ghosts,)),
            dma((bins,)),
            dma((bins,)),
            dma((bins,)),
            dma((bins,)),
        ],
        compiler_params=pltpu.CompilerParams(collective_id=0, has_side_effects=True),
    )(*arrays)
    return pl.pallas_call(
        store_body,
        name="dust_store",
        out_shape=tuple(jax.ShapeDtypeStruct(shape, jnp.float32) for shape in shapes),
        in_specs=[vmem] * 3,
        out_specs=(pl.BlockSpec(memory_space=pl.ANY),) * 3,
        scratch_shapes=[dma((3,))],
        compiler_params=pltpu.CompilerParams(vmem_limit_bytes=1 << 20),
    )(*results)


def solution(mesh):
    placed = (
        P("bin", "dom"),
        P(None, "bin", "dom"),
        P("dom"),
        P(None, "dom"),
        P(None, None, "dom"),
        P("dom"),
        P("dom"),
        P("bin"),
        P(None, "dom"),
        P("dom", None, None),
        P(),
        P(),
    )
    return jax.shard_map(
        body,
        mesh=mesh,
        in_specs=placed,
        out_specs=(P("bin", "dom"), P(None, "bin", "dom"), P(None, "dom")),
        check_vma=False,
    )
```
